32 devices in a mesh: dp: 8 (over z, x), row: 2 (over core), col: 2 (over y).
Axes of the slice: x: 2, y: 2, z: 4, core: 2. Of those that a mesh axis runs over, the one named last changes fastest.
Arguments:
- inputs: bfloat16 [32768, 576], P(('dp', 'row', 'col')), may hold values from -6 to 6
- seq_ids: int32 [32768], P(('dp', 'row', 'col')), may hold values from 0 to 127, as said below
- norm_one: float32 [576], replicated, may hold values from 0.25 to 1.75
- w_qkv: bfloat16 [576, 960], replicated, may hold values from -0.25 to 0.25
- w_out: bfloat16 [576, 576], replicated, may hold values from -1 to 1
- norm_two: float32 [576], replicated, may hold values from 0.25 to 1.75
- w_gate: bfloat16 [576, 1536], P('col', 'row'), may hold values from -0.25 to 0.25
- w_up: bfloat16 [576, 1536], P('col', 'row'), may hold values from -0.25 to 0.25
- w_down: bfloat16 [1536, 576], P('row', 'col'), may hold values from -0.3125 to 0.3125
- out_grad: bfloat16 [32768, 576], P(('dp', 'row', 'col')), may hold values from -6 to 6
Outputs:
- outputs: bfloat16 [32768, 576], P(('dp', 'row', 'col'))
- input_grad: float32 [32768, 576], P(('dp', 'row', 'col'))
- grad_norm_one: float32 [576], replicated
- grad_qkv: float32 [576, 960], replicated
- grad_out: float32 [576, 576], replicated
- grad_norm_two: float32 [576], replicated
- grad_gate: float32 [576, 1536], P('col', 'row')
- grad_up: float32 [576, 1536], P('col', 'row')
- grad_down: float32 [1536, 576], P('row', 'col')
The draws below stay inside these ranges and needn't reach their ends.
Inputs may be any that keep to these rules, and one draw needn't show every extreme that they name: `seq_ids`: within each block of 1024 consecutive tokens (the tokens of one device) the numbers start at 0 and rise by one where a new sequence starts; sequences start only at positions of the block that are multiples of 8; each sequence has 1 to 1024 tokens and lies inside one block; in some of the blocks (one at least), chosen from the seed, the first sequence has exactly 1024 tokens, and in one other block a sequence starts at every eighth position.
All inputs are finite; a program needn't handle non-finite values.
Results may differ from the reference program's by a relative error of at most 0.02.
Values may be sent and summed in bfloat16 or wider, within the bound.
No kernel may reach another device: no remote copies, remote signals or barrier semaphores. Data moves between devices by JAX's collectives and lax.ppermute only.
A program may use at most 192 MiB of HBM per device.

```python
import jax
import jax.numpy as jnp
from jax import lax

D = 576
HEADS = 9
KV_HEADS = 3
HEAD = 64
FF = 1536
QKV = 960
TOK_DEV = 1024
MAXLEN = 1024
TOKENS = 32768


def draw_seq_ids(key, part):
    blocks = TOKENS // TOK_DEV
    position = jnp.arange(TOK_DEV, dtype=jnp.int32)
    on_grid = (position % 8 == 0)[None, :]
    chance = jax.random.randint(jax.random.fold_in(key, 11), (blocks, TOK_DEV), 0, 24)
    shifts = 8 * jax.random.randint(jax.random.fold_in(key, 12), (blocks, 1), 0, MAXLEN // 8)
    ranking = jax.random.permutation(jax.random.fold_in(key, 13), blocks)
    single_seq = (ranking < max(blocks // 4, 1))[:, None]
    busy_block = (ranking == blocks - 1)[:, None]
    shifts = jnp.where(single_seq, 0, shifts)
    forced = ((position[None, :] + shifts) % MAXLEN == 0) | (position[None, :] == 0)
    random_start = on_grid & (chance == 0) & jnp.logical_not(single_seq & (position[None, :] < MAXLEN))
    starts = forced | random_start | busy_block & on_grid
    numbers = jnp.cumsum(starts.astype(jnp.int32), axis=1) - 1
    return numbers.reshape(TOKENS).astype(jnp.int32)


def block_levels(rng, dims, shards, low, largest):
    factor_of, own = 1.0, jax.random.fold_in(rng, 6)
    for dim, shards_of in shards:
        draws = jnp.exp(jax.random.uniform(jax.random.fold_in(own, dim), (shards_of,), jnp.float32, low / len(shards), largest / len(shards)))
        factor_of = factor_of * jnp.repeat(draws, dims[dim] // shards_of).reshape([-1 if axis == dim else 1 for axis in range(len(dims))])
    return factor_of


def normal_values(rng, shape, deviation, limit, shards=(), kind=jnp.bfloat16):
    entries = deviation * jax.random.normal(rng, shape, jnp.float32)
    if shards:
        entries = entries * block_levels(rng, shape, shards, -0.22, 0.18)
    return jnp.clip(entries, -limit, limit).astype(kind)


def setup_inputs(seed: int = 0) -> dict:
    streams_of = jax.random.split(jax.random.key(seed), 11)
    inputs = normal_values(streams_of[0], (TOKENS, D), 1.0, 6.0, ((0, 32),))
    seq_ids = draw_seq_ids(jax.random.fold_in(streams_of[10], 71), 0)
    norm_one = jnp.clip(1.0 + 0.15 * jax.random.normal(streams_of[2], (D,), jnp.float32), 0.25, 1.75)
    w_qkv = normal_values(streams_of[3], (D, QKV), D ** -0.5, 0.25)
    w_out = normal_values(streams_of[4], (D, D), (D // 16) ** -0.5, 1.0)
    norm_two = jnp.clip(1.0 + 0.15 * jax.random.normal(streams_of[5], (D,), jnp.float32), 0.25, 1.75)
    w_gate = normal_values(streams_of[6], (D, FF), D ** -0.5, 0.25, ((0, 2), (1, 2)))
    w_up = normal_values(streams_of[7], (D, FF), D ** -0.5, 0.25, ((0, 2), (1, 2)))
    w_down = normal_values(streams_of[8], (FF, D), (FF // 4) ** -0.5, 0.3125, ((0, 2), (1, 2)))
    out_grad = normal_values(streams_of[9], (TOKENS, D), 1.0, 6.0, ((0, 32),))
    return {"inputs": inputs, "seq_ids": seq_ids, "norm_one": norm_one, "w_qkv": w_qkv, "w_out": w_out, "norm_two": norm_two, "w_gate": w_gate, "w_up": w_up, "w_down": w_down, "out_grad": out_grad}


@jax.custom_vjp
def low(v):
    return lax.optimization_barrier(v.astype(jnp.bfloat16)).astype(jnp.float32)

@jax.custom_vjp
def low_back(v):
    return v

def low_keep(v):
    return (low(v), None)

def low_pass(kept, grad):
    return (grad,)

def back_keep(v):
    return (v, None)

def back_low(kept, grad):
    return (low(grad),)
low.defvjp(low_keep, low_pass)
low_back.defvjp(back_keep, back_low)
EPS = 1e-05
THETA = 100000.0
HIGH = lax.Precision.HIGHEST

def product(left_side, right_side):
    return jnp.dot(left_side, right_side, precision=HIGH, preferred_element_type=jnp.float32)

def places(seq_ids):
    token_count = seq_ids.shape[0]
    position = jnp.arange(token_count, dtype=jnp.int32)
    previous = jnp.concatenate([seq_ids[:1] - 1, seq_ids[:-1]])
    starts = jnp.where(seq_ids != previous, position, 0)
    return (position - lax.cummax(starts, axis=0)).astype(jnp.float32)

def tables(place, head_size):
    halfway = head_size // 2
    frequency = THETA ** (-2.0 * jnp.arange(halfway, dtype=jnp.float32) / head_size)
    angles = place[:, None] * frequency[None, :]
    return (jnp.cos(angles)[:, None, :], jnp.sin(angles)[:, None, :])

def rotate(values, cosine, sine_table):
    halfway = values.shape[-1] // 2
    front_half = values[..., :halfway]
    back_half = values[..., halfway:]
    return jnp.concatenate([front_half * cosine - back_half * sine_table, back_half * cosine + front_half * sine_table], axis=-1)

def rms_scale(values):
    return lax.rsqrt(lax.optimization_barrier(jnp.mean(values * values, axis=-1, keepdims=True)) + EPS)

def attend(query_heads, key_heads, value_heads, seq_ids):
    token_count = query_heads.shape[0]
    group_size = HEADS // KV_HEADS
    grouped = query_heads.reshape(token_count, KV_HEADS, group_size, HEAD)
    raw_dot = jnp.einsum('qgjd,kgd->gjqk', grouped, key_heads, precision=HIGH)
    scores = low_back(raw_dot) * HEAD ** (-0.5)
    position = jnp.arange(token_count, dtype=jnp.int32)
    allowed = (seq_ids[:, None] == seq_ids[None, :]) & (position[None, :] <= position[:, None])
    scores = jnp.where(allowed[None, None], scores, -1e+30)
    peak_score = lax.optimization_barrier(jnp.max(scores, axis=-1, keepdims=True))
    exponent = jnp.exp(scores - peak_score)
    attn_probs = low(exponent / lax.optimization_barrier(jnp.sum(exponent, axis=-1, keepdims=True)))
    mixed_rows = jnp.einsum('gjqk,kgd->qgjd', attn_probs, value_heads, precision=HIGH)
    return mixed_rows.reshape(token_count, HEADS * HEAD)

def forward(inputs, norm_one, w_qkv, w_out, norm_two, w_gate, w_up, w_down, seq_ids):
    token_count = inputs.shape[0]
    normed_one = low(inputs * rms_scale(inputs) * norm_one)
    joined_qkv = low_back(product(normed_one, w_qkv))
    query_width = HEADS * HEAD
    key_width = KV_HEADS * HEAD
    blocks = token_count // TOK_DEV
    query_part = joined_qkv[:, :query_width].reshape(blocks, TOK_DEV, HEADS, HEAD)
    key_part = joined_qkv[:, query_width:query_width + key_width].reshape(blocks, TOK_DEV, KV_HEADS, HEAD)
    value_part = joined_qkv[:, query_width + key_width:].reshape(blocks, TOK_DEV, KV_HEADS, HEAD)

    def one_block(pieces):
        query_rows, key_rows, value_rows, id_rows = pieces
        cosine, sine_table = tables(places(id_rows), HEAD)
        return attend(low(rotate(query_rows, cosine, sine_table)), low(rotate(key_rows, cosine, sine_table)), low(value_rows), id_rows)
    attended = lax.map(jax.checkpoint(one_block), (query_part, key_part, value_part, seq_ids.reshape(blocks, TOK_DEV)))
    attended = low_back(low(attended.reshape(token_count, query_width)))
    middle = inputs + low_back(product(attended, w_out))
    normed_two = low(middle * rms_scale(middle) * norm_two)
    gate_pre = low_back(product(normed_two, w_gate))
    up_pre = low_back(product(normed_two, w_up))
    hidden = low_back(low(gate_pre * jax.nn.sigmoid(gate_pre) * up_pre))
    return middle + low_back(product(hidden, w_down))

def reference(inputs, seq_ids, norm_one, w_qkv, w_out, norm_two, w_gate, w_up, w_down, out_grad):
    floats = (inputs.astype(jnp.float32), norm_one.astype(jnp.float32), w_qkv.astype(jnp.float32), w_out.astype(jnp.float32), norm_two.astype(jnp.float32), w_gate.astype(jnp.float32), w_up.astype(jnp.float32), w_down.astype(jnp.float32))

    def wrapped(inputs_f, gain_one, qkv_f, out_f, gain_two, gate_f, up_f, down_f):
        return forward(inputs_f, gain_one, qkv_f, out_f, gain_two, gate_f, up_f, down_f, seq_ids)
    result, pullback = jax.vjp(wrapped, *floats)
    grads_all = pullback(out_grad.astype(jnp.float32))
    return (result.astype(jnp.bfloat16), grads_all[0], grads_all[1], grads_all[2], grads_all[3], grads_all[4], grads_all[5], grads_all[6], grads_all[7])
```

```python
import functools

import jax
import jax.numpy as jnp
from jax import lax
from jax.experimental import pallas as pl
from jax.experimental.pallas import tpu as pltpu
from jax.sharding import PartitionSpec as P

HEADS = 9
KV_HEADS = 3
GROUP = HEADS // KV_HEADS
HEAD = 64
BLOCK = 256
LANES = 128
LOG2E = 1.4426950408889634
EPS = 1e-05
THETA = 100000.0
NEG = -1e30
F32 = jnp.float32
BF16 = jnp.bfloat16


def dot_nn(a, b):
    return lax.dot_general(a, b, (((1,), (0,)), ((), ())), preferred_element_type=F32)


def dot_nt(a, b):
    return lax.dot_general(a, b, (((1,), (1,)), ((), ())), preferred_element_type=F32)


def dot_tn(a, b):
    return lax.dot_general(a, b, (((0,), (0,)), ((), ())), preferred_element_type=F32)


def partner_lanes(x):
    lane = lax.broadcasted_iota(jnp.int32, x.shape, 1)
    front = lax.rem(lane, HEAD) < HEAD // 2
    return jnp.where(
        front, pltpu.roll(x, LANES - HEAD // 2, 1), pltpu.roll(x, HEAD // 2, 1)
    )


def allowed_tile(start_row, key_start, query_start, diagonal):
    shape = (BLOCK, start_row.shape[1])
    keys = key_start + lax.broadcasted_iota(jnp.int32, shape, 0)
    mask = keys >= start_row
    if diagonal:
        rows = query_start + lax.rem(lax.broadcasted_iota(jnp.int32, shape, 1), BLOCK)
        mask = mask & (keys <= rows)
    return mask


def front_kernel(
    inputs_ref, start_ref, cos_ref, sin_ref, norm_ref, w_qkv_ref, w_out_ref,
    q_ref, k_ref, v_ref, lse_ref, att_ref, mid_ref,
    k_all, vt_all, acc, stat_m, stat_l,
):
    i = pl.program_id(0)
    x = inputs_ref[...].astype(F32)
    scale = lax.rsqrt(jnp.mean(x * x, axis=-1, keepdims=True) + EPS)
    normed = (x * scale * norm_ref[...]).astype(BF16)
    joined = dot_nn(normed, w_qkv_ref[...])
    width = (HEADS + KV_HEADS) * HEAD
    cosine, sine = cos_ref[...], sin_ref[...]
    for c in range(width // LANES):
        part = joined[:, c * LANES:(c + 1) * LANES]
        turned = (part * cosine + partner_lanes(part) * sine).astype(BF16)
        for half in range(2):
            h = 2 * c + half
            piece = turned[:, half * HEAD:(half + 1) * HEAD]
            if h < HEADS:
                q_ref[h] = piece * BF16(HEAD ** -0.5)
            else:
                k_ref[h - HEADS] = piece
                k_all[h - HEADS, pl.ds(pl.multiple_of(i * BLOCK, BLOCK), BLOCK), :] = piece
    values = joined[:, width:]
    values_t = values.T.astype(BF16)
    for g in range(KV_HEADS):
        v_ref[g] = values[:, g * HEAD:(g + 1) * HEAD].astype(BF16)
        vt_all[g, i] = values_t[g * HEAD:(g + 1) * HEAD, :]
    start = start_ref[...]
    start_row = jnp.concatenate([start] * GROUP, axis=1)
    stat_m[...] = jnp.full(stat_m.shape, NEG, F32)
    stat_l[...] = jnp.zeros(stat_l.shape, F32)
    acc[...] = jnp.zeros(acc.shape, F32)

    def tile(j, diagonal):
        mask = allowed_tile(start_row, j * BLOCK, i * BLOCK, diagonal)
        for g in range(KV_HEADS):
            queries = q_ref[g * GROUP:(g + 1) * GROUP].reshape(GROUP * BLOCK, HEAD)
            keys = k_all[g, pl.ds(pl.multiple_of(j * BLOCK, BLOCK), BLOCK), :]
            scores = jnp.where(mask, dot_nt(keys, queries) * LOG2E, NEG)
            peak_old = stat_m[g:g + 1]
            peak = jnp.maximum(peak_old, jnp.max(scores, axis=0, keepdims=True))
            expo = jnp.exp2(scores - peak)
            expo = jnp.where(mask, expo, 0.0)
            fade = jnp.exp2(peak_old - peak)
            stat_m[g:g + 1] = peak
            stat_l[g:g + 1] = stat_l[g:g + 1] * fade + jnp.sum(expo, axis=0, keepdims=True)
            acc[g] = acc[g] * fade + dot_nn(vt_all[g, j], expo.astype(BF16))

    def step(j, carry):
        tile(j, False)
        return carry

    lax.fori_loop(0, i, step, 0)
    tile(i, True)
    pieces = []
    for g in range(KV_HEADS):
        total = stat_l[g:g + 1]
        mixed = acc[g] / total
        logsum = stat_m[g:g + 1] + jnp.log2(total)
        for h in range(GROUP):
            lse_ref[g * GROUP + h:g * GROUP + h + 1, :] = logsum[:, h * BLOCK:(h + 1) * BLOCK]
            pieces.append(mixed[:, h * BLOCK:(h + 1) * BLOCK])
    attended = jnp.concatenate(pieces, axis=0).T.astype(BF16)
    att_ref[...] = attended
    mid_ref[...] = x + dot_nn(attended, w_out_ref[...])


def front(inputs, start, cosine, sine, norm_one, w_qkv, w_out):
    tokens, width = inputs.shape
    blocks = tokens // BLOCK
    whole = lambda i: (0, 0)
    rows = lambda i: (i, 0)
    return pl.pallas_call(
        front_kernel,
        grid=(blocks,),
        in_specs=[
            pl.BlockSpec((BLOCK, width), rows),
            pl.BlockSpec((1, BLOCK), lambda i: (0, i)),
            pl.BlockSpec((BLOCK, LANES), rows),
            pl.BlockSpec((BLOCK, LANES), rows),
            pl.BlockSpec((1, width), whole),
            pl.BlockSpec(w_qkv.shape, whole),
            pl.BlockSpec(w_out.shape, whole),
        ],
        out_specs=[
            pl.BlockSpec((HEADS, BLOCK, HEAD), lambda i: (0, i, 0)),
            pl.BlockSpec((KV_HEADS, BLOCK, HEAD), lambda i: (0, i, 0)),
            pl.BlockSpec((KV_HEADS, BLOCK, HEAD), lambda i: (0, i, 0)),
            pl.BlockSpec((16, BLOCK), lambda i: (0, i)),
            pl.BlockSpec((BLOCK, width), rows),
            pl.BlockSpec((BLOCK, width), rows),
        ],
        out_shape=[
            jax.ShapeDtypeStruct((HEADS, tokens, HEAD), BF16),
            jax.ShapeDtypeStruct((KV_HEADS, tokens, HEAD), BF16),
            jax.ShapeDtypeStruct((KV_HEADS, tokens, HEAD), BF16),
            jax.ShapeDtypeStruct((16, tokens), F32),
            jax.ShapeDtypeStruct((tokens, width), BF16),
            jax.ShapeDtypeStruct((tokens, width), F32),
        ],
        scratch_shapes=[
            pltpu.VMEM((KV_HEADS, tokens, HEAD), BF16),
            pltpu.VMEM((KV_HEADS, blocks, HEAD, BLOCK), BF16),
            pltpu.VMEM((KV_HEADS, HEAD, GROUP * BLOCK), F32),
            pltpu.VMEM((8, GROUP * BLOCK), F32),
            pltpu.VMEM((8, GROUP * BLOCK), F32),
        ],
        cost_estimate=pl.CostEstimate(flops=6 * 10**9, bytes_accessed=12 * 10**6, transcendentals=6 * 10**6),
        name="front",
    )(inputs, start, cosine, sine, norm_one, w_qkv, w_out)


def mlp_kernel(
    place_ref, mid_ref, og_ref, att_ref, norm_ref, w_out_ref, own_ref, side_ref, row_ref, far_ref, sel_ref,
    out_ref, mg_ref, do_ref, delta_ref, g3_ref, gout_ref, gain_ref,
    weights, acc3, acc_out, acc_gain,
):
    i = pl.program_id(0)
    rows_half, cols_half = own_ref.shape[1], own_ref.shape[2]
    col, row = place_ref[0], place_ref[1]

    @pl.when(i == 0)
    def _():
        for ref, c, r in ((own_ref, col, row), (side_ref, 1 - col, row), (row_ref, col, 1 - row), (far_ref, 1 - col, 1 - row)):
            at_row = pl.multiple_of(c * rows_half, 32)
            at_col = pl.multiple_of(r * cols_half, LANES)
            for t in range(3):
                weights[t, pl.ds(at_row, rows_half), pl.ds(at_col, cols_half)] = ref[t]
        acc3[...] = jnp.zeros(acc3.shape, F32)
        acc_out[...] = jnp.zeros(acc_out.shape, F32)
        acc_gain[...] = jnp.zeros(acc_gain.shape, F32)

    middle = mid_ref[...]
    og = og_ref[...]
    gain = norm_ref[...]
    scale = lax.rsqrt(jnp.mean(middle * middle, axis=-1, keepdims=True) + EPS)
    normed = (middle * scale * gain).astype(BF16)
    og_t = og.astype(F32).T.astype(BF16)
    normed_t = normed.astype(F32).T.astype(BF16)
    chunk = cols_half // 2
    mlp_out = jnp.zeros(middle.shape, F32)
    normed_grad = jnp.zeros(middle.shape, F32)
    for c in range(2 * cols_half // chunk):
        at = slice(c * chunk, (c + 1) * chunk)
        gate_pre = dot_nn(normed, weights[0, :, at])
        up_pre = dot_nn(normed, weights[1, :, at])
        hidden_low = dot_nn(og, weights[2, :, at]).astype(BF16).astype(F32)
        squashed = 1.0 / (1.0 + jnp.exp(-gate_pre))
        active = gate_pre * squashed
        hidden = (active * up_pre).astype(BF16)
        gate_low = (hidden_low * up_pre * squashed * (1.0 + gate_pre * (1.0 - squashed))).astype(BF16)
        up_low = (hidden_low * active).astype(BF16)
        mlp_out += dot_nt(hidden, weights[2, :, at])
        normed_grad += dot_nt(gate_low, weights[0, :, at]) + dot_nt(up_low, weights[1, :, at])
        acc3[0, :, at] += dot_nn(normed_t, gate_low)
        acc3[1, :, at] += dot_nn(normed_t, up_low)
        acc3[2, :, at] += dot_nn(og_t, hidden)
    out_ref[...] = (middle + mlp_out).astype(BF16)
    acc_gain[...] += jnp.sum((normed_grad * middle * scale).reshape(BLOCK // 8, 8, middle.shape[1]), axis=0)
    weighted = normed_grad * gain
    inner = jnp.sum(weighted * middle, axis=-1, keepdims=True)
    middle_grad = (
        og.astype(F32) + scale * weighted
        - middle * (scale * scale * scale) * inner / middle.shape[1]
    )
    mg_ref[...] = middle_grad
    middle_low = middle_grad.astype(BF16)
    attended = att_ref[...]
    acc_out[...] += dot_tn(attended, middle_low)
    att_low = dot_nt(middle_low, w_out_ref[...]).astype(BF16)
    for h in range(HEADS):
        do_ref[h] = att_low[:, h * HEAD:(h + 1) * HEAD]
    product = att_low.astype(F32) * attended.astype(F32)
    coarse = product.astype(BF16)
    fine = (product - coarse.astype(F32)).astype(BF16)
    delta_ref[...] = dot_nt(sel_ref[...], coarse) + dot_nt(sel_ref[...], fine)

    @pl.when(i == pl.num_programs(0) - 1)
    def _():
        for r in range(2):
            for c in range(2):
                for t in range(3):
                    for part in range(cols_half // LANES):
                        lane = r * cols_half + part * LANES
                        g3_ref[r, c, t, part] = acc3[t, c * rows_half:(c + 1) * rows_half, lane:lane + LANES].astype(BF16)
        gout_ref[...] = acc_out[...].astype(BF16)
        gain_ref[...] = acc_gain[...]


def mlp(place, middle, out_grad, attended, norm_two, w_out, own, side, across, far, selector):
    tokens, width = middle.shape
    rows_half, cols_half = own.shape[1:]
    blocks = tokens // BLOCK
    parts = cols_half // LANES
    rows = lambda i: (i, 0)
    whole = lambda i: (0, 0)
    whole3 = lambda i: (0, 0, 0)
    once = pl.Buffered(1)
    return pl.pallas_call(
        mlp_kernel,
        grid=(blocks,),
        in_specs=[
            pl.BlockSpec(memory_space=pltpu.SMEM),
            pl.BlockSpec((BLOCK, width), rows),
            pl.BlockSpec((BLOCK, width), rows),
            pl.BlockSpec((BLOCK, width), rows),
            pl.BlockSpec((1, width), whole),
            pl.BlockSpec(w_out.shape, whole, pipeline_mode=once),
            pl.BlockSpec(own.shape, whole3, pipeline_mode=once),
            pl.BlockSpec(own.shape, whole3, pipeline_mode=once),
            pl.BlockSpec(own.shape, whole3, pipeline_mode=once),
            pl.BlockSpec(own.shape, whole3, pipeline_mode=once),
            pl.BlockSpec(selector.shape, whole),
        ],
        out_specs=[
            pl.BlockSpec((BLOCK, width), rows),
            pl.BlockSpec((BLOCK, width), rows),
            pl.BlockSpec((HEADS, BLOCK, HEAD), lambda i: (0, i, 0)),
            pl.BlockSpec((16, BLOCK), lambda i: (0, i)),
            pl.BlockSpec((2, 2, 3, parts, rows_half, LANES), lambda i: (0,) * 6, pipeline_mode=once),
            pl.BlockSpec(w_out.shape, whole, pipeline_mode=once),
            pl.BlockSpec((8, width), whole),
        ],
        out_shape=[
            jax.ShapeDtypeStruct((tokens, width), BF16),
            jax.ShapeDtypeStruct((tokens, width), F32),
            jax.ShapeDtypeStruct((HEADS, tokens, HEAD), BF16),
            jax.ShapeDtypeStruct((16, tokens), F32),
            jax.ShapeDtypeStruct((2, 2, 3, parts, rows_half, LANES), BF16),
            jax.ShapeDtypeStruct(w_out.shape, BF16),
            jax.ShapeDtypeStruct((8, width), F32),
        ],
        scratch_shapes=[
            pltpu.VMEM((3, 2 * rows_half, 2 * cols_half), BF16),
            pltpu.VMEM((3, 2 * rows_half, 2 * cols_half), F32),
            pltpu.VMEM(w_out.shape, F32),
            pltpu.VMEM((8, width), F32),
        ],
        cost_estimate=pl.CostEstimate(flops=18 * 10**9, bytes_accessed=24 * 10**6, transcendentals=2 * 10**6),
        name="mlp",
    )(place, middle, out_grad, attended, norm_two, w_out, own, side, across, far, selector)


def back_kernel(
    q_ref, k_ref, v_ref, do_ref, lse_ref, delta_ref, start_ref, cos_ref, sin_ref,
    inputs_ref, mg_ref, norm_ref, w_qkv_ref,
    ig_ref, gqkv_ref, gain_ref,
    dq_all, dk, dv, acc_qkv, acc_gain,
):
    j = pl.program_id(0)
    blocks = pl.num_programs(0)

    @pl.when(j == 0)
    def _():
        dq_all[...] = jnp.zeros(dq_all.shape, F32)
        acc_qkv[...] = jnp.zeros(acc_qkv.shape, F32)
        acc_gain[...] = jnp.zeros(acc_gain.shape, F32)

    dk[...] = jnp.zeros(dk.shape, F32)
    dv[...] = jnp.zeros(dv.shape, F32)
    keys_t = [k_ref[g].astype(F32).T.astype(BF16) for g in range(KV_HEADS)]

    def tile(i, diagonal):
        at = pl.multiple_of(i * BLOCK, BLOCK)
        span = pl.ds(at, BLOCK)
        start_row = jnp.concatenate([start_ref[:, span]] * GROUP, axis=1)
        mask = allowed_tile(start_row, j * BLOCK, i * BLOCK, diagonal)
        for g in range(KV_HEADS):
            heads = range(g * GROUP, (g + 1) * GROUP)
            queries = q_ref[g * GROUP:(g + 1) * GROUP, span, :].reshape(GROUP * BLOCK, HEAD)
            grads = do_ref[g * GROUP:(g + 1) * GROUP, span, :].reshape(GROUP * BLOCK, HEAD)
            lse_row = jnp.concatenate([lse_ref[h:h + 1, span] for h in heads], axis=1)
            delta_row = jnp.concatenate([delta_ref[h:h + 1, span] for h in heads], axis=1)
            keys, values = k_ref[g], v_ref[g]
            soft = jnp.where(mask, jnp.exp2(dot_nt(keys, queries) * LOG2E - lse_row), 0.0)
            prob_grad = dot_nt(values, grads)
            score_low = (soft * (prob_grad - delta_row)).astype(BF16)
            dv[g] += dot_nn(soft.astype(BF16), grads)
            dk[g] += dot_nn(score_low, queries)
            dq_all[i, g] += dot_nn(keys_t[g], score_low)

    def step(i, carry):
        tile(i, False)
        return carry

    tile(j, True)
    lax.fori_loop(j + 1, blocks, step, 0)

    cosine, sine = cos_ref[...], sin_ref[...]
    pieces = []
    for g in range(KV_HEADS):
        part = dq_all[j, g] * (HEAD ** -0.5)
        pieces += [part[:, h * BLOCK:(h + 1) * BLOCK] for h in range(GROUP)]
    query_grad = jnp.concatenate(pieces, axis=0).T
    turned = jnp.concatenate([query_grad, dk[0], dk[1], dk[2]], axis=1)
    columns = []
    for c in range(turned.shape[1] // LANES):
        part = turned[:, c * LANES:(c + 1) * LANES]
        columns.append((part * cosine - partner_lanes(part) * sine).astype(BF16))
    values_low = jnp.concatenate([dv[0], dv[1], dv[2]], axis=1).astype(BF16)
    joined_low = jnp.concatenate(columns + [values_low], axis=1)

    x = inputs_ref[...].astype(F32)
    gain = norm_ref[...]
    scale = lax.rsqrt(jnp.mean(x * x, axis=-1, keepdims=True) + EPS)
    normed = (x * scale * gain).astype(BF16)
    acc_qkv[...] += dot_tn(normed, joined_low)
    normed_grad = dot_nt(joined_low, w_qkv_ref[...])
    acc_gain[...] += jnp.sum((normed_grad * x * scale).reshape(BLOCK // 8, 8, x.shape[1]), axis=0)
    weighted = normed_grad * gain
    inner = jnp.sum(weighted * x, axis=-1, keepdims=True)
    ig_ref[...] = mg_ref[...] + scale * weighted - x * (scale * scale * scale) * inner / x.shape[1]

    @pl.when(j == blocks - 1)
    def _():
        gqkv_ref[...] = acc_qkv[...].astype(BF16)
        gain_ref[...] = acc_gain[...]


def back(q, k, v, do, lse, delta, start, cosine, sine, inputs, middle_grad, norm_one, w_qkv):
    tokens, width = inputs.shape
    blocks = tokens // BLOCK
    rows = lambda j: (j, 0)
    whole = lambda j: (0, 0)
    whole3 = lambda j: (0, 0, 0)
    mine3 = lambda j: (0, j, 0)
    return pl.pallas_call(
        back_kernel,
        grid=(blocks,),
        in_specs=[
            pl.BlockSpec(q.shape, whole3),
            pl.BlockSpec((KV_HEADS, BLOCK, HEAD), mine3),
            pl.BlockSpec((KV_HEADS, BLOCK, HEAD), mine3),
            pl.BlockSpec(do.shape, whole3),
            pl.BlockSpec(lse.shape, whole),
            pl.BlockSpec(delta.shape, whole),
            pl.BlockSpec(start.shape, whole),
            pl.BlockSpec((BLOCK, LANES), rows),
            pl.BlockSpec((BLOCK, LANES), rows),
            pl.BlockSpec((BLOCK, width), rows),
            pl.BlockSpec((BLOCK, width), rows),
            pl.BlockSpec((1, width), whole),
            pl.BlockSpec(w_qkv.shape, whole),
        ],
        out_specs=[
            pl.BlockSpec((BLOCK, width), rows),
            pl.BlockSpec(w_qkv.shape, whole),
            pl.BlockSpec((8, width), whole),
        ],
        out_shape=[
            jax.ShapeDtypeStruct((tokens, width), F32),
            jax.ShapeDtypeStruct(w_qkv.shape, BF16),
            jax.ShapeDtypeStruct((8, width), F32),
        ],
        scratch_shapes=[
            pltpu.VMEM((blocks, KV_HEADS, HEAD, GROUP * BLOCK), F32),
            pltpu.VMEM((KV_HEADS, BLOCK, HEAD), F32),
            pltpu.VMEM((KV_HEADS, BLOCK, HEAD), F32),
            pltpu.VMEM(w_qkv.shape, F32),
            pltpu.VMEM((8, width), F32),
        ],
        cost_estimate=pl.CostEstimate(flops=8 * 10**9, bytes_accessed=16 * 10**6, transcendentals=6 * 10**6),
        name="back",
    )(q, k, v, do, lse, delta, start, cosine, sine, inputs, middle_grad, norm_one, w_qkv)


def places(seq_ids):
    position = jnp.arange(seq_ids.shape[0], dtype=jnp.int32)
    previous = jnp.concatenate([seq_ids[:1] - 1, seq_ids[:-1]])
    start = lax.cummax(jnp.where(seq_ids != previous, position, 0), axis=0)
    return start, (position - start).astype(F32)


def tables(place):
    half = HEAD // 2
    frequency = THETA ** (-2.0 * jnp.arange(half, dtype=F32) / HEAD)
    angles = frequency[:, None] * place[None, :]
    cosine, sine = jnp.cos(angles).T, jnp.sin(angles).T
    copies = LANES // HEAD
    return (
        jnp.concatenate([cosine, cosine] * copies, axis=1),
        jnp.concatenate([-sine, sine] * copies, axis=1),
    )


SWAP = [(0, 1), (1, 0)]


def halve(data, axis, bit, size):
    pairs = [(n, n ^ bit) for n in range(size)]
    mine = (lax.axis_index(axis) // bit) % 2
    halves = data.reshape((2, data.shape[0] // 2) + data.shape[1:])
    sent = lax.dynamic_index_in_dim(halves, 1 - mine, 0, keepdims=False)
    kept = lax.dynamic_index_in_dim(halves, mine, 0, keepdims=False)
    arrived = lax.ppermute(sent, axis, pairs)
    return (kept.astype(F32) + arrived.astype(F32)).astype(BF16)


def double(data, axis, bit, size):
    pairs = [(n, n ^ bit) for n in range(size)]
    mine = (lax.axis_index(axis) // bit) % 2
    arrived = lax.ppermute(data, axis, pairs)
    lower = mine == 0
    return jnp.concatenate([jnp.where(lower, data, arrived), jnp.where(lower, arrived, data)], axis=0)


def bits(size):
    out, bit = [], 1
    while bit < size:
        out.append(bit)
        bit *= 2
    return out


def per_device(inputs, seq_ids, norm_one, w_qkv, w_out, norm_two, w_gate, w_up, w_down, out_grad):
    dp_size, row_size, col_size = (lax.axis_size(name) for name in ("dp", "row", "col"))
    width = inputs.shape[1]
    own = jnp.stack([w_gate, w_up, w_down.T])
    side = lax.ppermute(own, "col", SWAP)
    across = lax.ppermute(own, "row", SWAP)
    far = lax.ppermute(side, "row", SWAP)
    start, place = places(seq_ids)
    start = start[None, :]
    cosine, sine = tables(place)
    gain_one, gain_two = norm_one[None, :], norm_two[None, :]
    q, k, v, lse, attended, middle = front(inputs, start, cosine, sine, gain_one, w_qkv, w_out)
    selector = (jnp.arange(16)[:, None] == jnp.arange(width)[None, :] // HEAD).astype(BF16)
    spot = jnp.stack([lax.axis_index("col"), lax.axis_index("row")]).astype(jnp.int32)
    outputs, middle_grad, do, delta, grads, gout, gain_two_part = mlp(
        spot, middle, out_grad, attended, gain_two, w_out, own, side, across, far, selector
    )
    grads = grads.reshape(-1, LANES)
    grads = halve(grads, "row", 1, row_size)
    grads = halve(grads, "col", 1, col_size)
    for bit in bits(dp_size):
        grads = halve(grads, "dp", bit, dp_size)
    for bit in reversed(bits(dp_size)):
        grads = double(grads, "dp", bit, dp_size)
    input_grad, gqkv, gain_one_part = back(
        q, k, v, do, lse, delta, start, cosine, sine, inputs, middle_grad, gain_one, w_qkv
    )
    gains = lax.psum((jnp.sum(gain_one_part, axis=0), jnp.sum(gain_two_part, axis=0)), ("dp", "row", "col"))
    shared = jnp.concatenate([gqkv.reshape(-1, LANES), gout.reshape(-1, LANES)], axis=0)
    extra = -shared.shape[0] % (8 * dp_size * row_size * col_size)
    rows_shared = shared.shape[0]
    shared = jnp.pad(shared, ((0, extra), (0, 0)))
    shared = halve(shared, "row", 1, row_size)
    shared = halve(shared, "col", 1, col_size)
    for bit in bits(dp_size):
        shared = halve(shared, "dp", bit, dp_size)
    for bit in reversed(bits(dp_size)):
        shared = double(shared, "dp", bit, dp_size)
    shared = double(shared, "col", 1, col_size)
    shared = double(shared, "row", 1, row_size)
    cut = gqkv.size // LANES
    grad_qkv = shared[:cut].reshape(gqkv.shape).astype(F32)
    grad_out = shared[cut:rows_shared].reshape(gout.shape).astype(F32)
    parts = w_gate.shape[1] // LANES
    grads = grads.reshape(3, parts, w_gate.shape[0], LANES).astype(F32)
    grad_gate = grads[0].transpose(1, 0, 2).reshape(w_gate.shape)
    grad_up = grads[1].transpose(1, 0, 2).reshape(w_up.shape)
    grad_down = grads[2].transpose(0, 2, 1).reshape(w_down.shape)
    return (outputs, input_grad, gains[0], grad_qkv, grad_out, gains[1], grad_gate, grad_up, grad_down)


def solution(mesh):
    tokens = P(("dp", "row", "col"), None)
    grid, turned = P("col", "row"), P("row", "col")
    return jax.shard_map(
        per_device,
        mesh=mesh,
        in_specs=(tokens, P(("dp", "row", "col")), P(), P(), P(), P(), grid, grid, turned, tokens),
        out_specs=(tokens, tokens, P(), P(), P(), P(), grid, grid, turned),
        check_vma=False,
    )
```

```python
import functools

import jax
import jax.numpy as jnp
from jax import lax
from jax.experimental import pallas as pl
from jax.experimental.pallas import tpu as pltpu
from jax.sharding import PartitionSpec as P


HEADS = 9
KV_HEADS = 3
GROUP = HEADS // KV_HEADS
HEAD = 64
BLOCK = 256
LANES = 128
LOG2E = 1.4426950408889634
EPS = 1e-05
THETA = 100000.0
NEG = -1e30
F32 = jnp.float32
BF16 = jnp.bfloat16


def dot_nn(a, b):
    return lax.dot_general(a, b, (((1,), (0,)), ((), ())), preferred_element_type=F32)


def dot_nt(a, b):
    return lax.dot_general(a, b, (((1,), (1,)), ((), ())), preferred_element_type=F32)


def dot_tn(a, b):
    return lax.dot_general(a, b, (((0,), (0,)), ((), ())), preferred_element_type=F32)


def partner_lanes(x):
    lane = lax.broadcasted_iota(jnp.int32, x.shape, 1)
    front = lax.rem(lane, HEAD) < HEAD // 2
    return jnp.where(
        front, pltpu.roll(x, LANES - HEAD // 2, 1), pltpu.roll(x, HEAD // 2, 1)
    )


def allowed_tile(start_row, key_start, query_start, diagonal):
    shape = (BLOCK, start_row.shape[1])
    keys = key_start + lax.broadcasted_iota(jnp.int32, shape, 0)
    mask = keys >= start_row
    if diagonal:
        rows = query_start + lax.rem(lax.broadcasted_iota(jnp.int32, shape, 1), BLOCK)
        mask = mask & (keys <= rows)
    return mask


def front_kernel(
    inputs_ref, start_ref, cos_ref, sin_ref, norm_ref, w_qkv_ref, w_out_ref,
    q_ref, k_ref, v_ref, lse_ref, att_ref, mid_ref, normed_ref,
    k_all, vt_all, acc, stat_m, stat_l,
):
    i = pl.program_id(0)
    x = inputs_ref[...].astype(F32)
    scale = lax.rsqrt(jnp.mean(x * x, axis=-1, keepdims=True) + EPS)
    normed = (x * scale * norm_ref[...]).astype(BF16)
    normed_ref[...] = normed
    joined = dot_nn(normed, w_qkv_ref[...])
    width = (HEADS + KV_HEADS) * HEAD
    cosine, sine = cos_ref[...], sin_ref[...]
    for c in range(width // LANES):
        part = joined[:, c * LANES:(c + 1) * LANES]
        turned = (part * cosine + partner_lanes(part) * sine).astype(BF16)
        for half in range(2):
            h = 2 * c + half
            piece = turned[:, half * HEAD:(half + 1) * HEAD]
            if h < HEADS:
                q_ref[h] = piece * BF16(HEAD ** -0.5)
            else:
                k_ref[h - HEADS] = piece
                k_all[h - HEADS, pl.ds(pl.multiple_of(i * BLOCK, BLOCK), BLOCK), :] = piece
    values = joined[:, width:]
    values_t = values.T.astype(BF16)
    for g in range(KV_HEADS):
        v_ref[g] = values[:, g * HEAD:(g + 1) * HEAD].astype(BF16)
        vt_all[g, i] = values_t[g * HEAD:(g + 1) * HEAD, :]
    start = start_ref[...]
    start_row = jnp.concatenate([start] * GROUP, axis=1)
    stat_m[...] = jnp.full(stat_m.shape, NEG, F32)
    stat_l[...] = jnp.zeros(stat_l.shape, F32)
    acc[...] = jnp.zeros(acc.shape, F32)

    def tile(j, diagonal):
        mask = allowed_tile(start_row, j * BLOCK, i * BLOCK, diagonal)
        for g in range(KV_HEADS):
            queries = q_ref[g * GROUP:(g + 1) * GROUP].reshape(GROUP * BLOCK, HEAD)
            keys = k_all[g, pl.ds(pl.multiple_of(j * BLOCK, BLOCK), BLOCK), :]
            scores = jnp.where(mask, dot_nt(keys, queries) * LOG2E, NEG)
            peak_old = stat_m[g:g + 1]
            peak = jnp.maximum(peak_old, jnp.max(scores, axis=0, keepdims=True))
            expo = jnp.exp2(scores - peak)
            expo = jnp.where(mask, expo, 0.0)
            fade = jnp.exp2(peak_old - peak)
            stat_m[g:g + 1] = peak
            stat_l[g:g + 1] = stat_l[g:g + 1] * fade + jnp.sum(expo, axis=0, keepdims=True)
            acc[g] = acc[g] * fade + dot_nn(vt_all[g, j], expo.astype(BF16))

    def step(j, carry):
        tile(j, False)
        return carry

    lax.fori_loop(0, i, step, 0)
    tile(i, True)
    pieces = []
    for g in range(KV_HEADS):
        total = stat_l[g:g + 1]
        mixed = acc[g] / total
        logsum = stat_m[g:g + 1] + jnp.log2(total)
        for h in range(GROUP):
            lse_ref[g * GROUP + h:g * GROUP + h + 1, :] = logsum[:, h * BLOCK:(h + 1) * BLOCK]
            pieces.append(mixed[:, h * BLOCK:(h + 1) * BLOCK])
    attended = jnp.concatenate(pieces, axis=0).T.astype(BF16)
    att_ref[...] = attended
    mid_ref[...] = x + dot_nn(attended, w_out_ref[...])


def front(inputs, start, cosine, sine, norm_one, w_qkv, w_out):
    tokens, width = inputs.shape
    blocks = tokens // BLOCK
    whole = lambda i: (0, 0)
    rows = lambda i: (i, 0)
    return pl.pallas_call(
        front_kernel,
        grid=(blocks,),
        in_specs=[
            pl.BlockSpec((BLOCK, width), rows),
            pl.BlockSpec((1, BLOCK), lambda i: (0, i)),
            pl.BlockSpec((BLOCK, LANES), rows),
            pl.BlockSpec((BLOCK, LANES), rows),
            pl.BlockSpec((1, width), whole),
            pl.BlockSpec(w_qkv.shape, whole),
            pl.BlockSpec(w_out.shape, whole),
        ],
        out_specs=[
            pl.BlockSpec((HEADS, BLOCK, HEAD), lambda i: (0, i, 0)),
            pl.BlockSpec((KV_HEADS, BLOCK, HEAD), lambda i: (0, i, 0)),
            pl.BlockSpec((KV_HEADS, BLOCK, HEAD), lambda i: (0, i, 0)),
            pl.BlockSpec((16, BLOCK), lambda i: (0, i)),
            pl.BlockSpec((BLOCK, width), rows),
            pl.BlockSpec((BLOCK, width), rows),
            pl.BlockSpec((BLOCK, width), rows),
        ],
        out_shape=[
            jax.ShapeDtypeStruct((HEADS, tokens, HEAD), BF16),
            jax.ShapeDtypeStruct((KV_HEADS, tokens, HEAD), BF16),
            jax.ShapeDtypeStruct((KV_HEADS, tokens, HEAD), BF16),
            jax.ShapeDtypeStruct((16, tokens), F32),
            jax.ShapeDtypeStruct((tokens, width), BF16),
            jax.ShapeDtypeStruct((tokens, width), F32),
            jax.ShapeDtypeStruct((tokens, width), BF16),
        ],
        scratch_shapes=[
            pltpu.VMEM((KV_HEADS, tokens, HEAD), BF16),
            pltpu.VMEM((KV_HEADS, blocks, HEAD, BLOCK), BF16),
            pltpu.VMEM((KV_HEADS, HEAD, GROUP * BLOCK), F32),
            pltpu.VMEM((8, GROUP * BLOCK), F32),
            pltpu.VMEM((8, GROUP * BLOCK), F32),
        ],
        cost_estimate=pl.CostEstimate(flops=6 * 10**9, bytes_accessed=12 * 10**6, transcendentals=6 * 10**6),
        name="front",
    )(inputs, start, cosine, sine, norm_one, w_qkv, w_out)


def place_weights(place_ref, blocks, weights):
    rows_half, cols_half = blocks[0].shape[1:]
    col, row = place_ref[0], place_ref[1]
    spots = ((col, row), (1 - col, row), (col, 1 - row), (1 - col, 1 - row))
    for ref, (c, r) in zip(blocks, spots):
        at_row = pl.multiple_of(c * rows_half, 32)
        at_col = pl.multiple_of(r * cols_half, LANES)
        for t in range(weights.shape[0]):
            weights[t, pl.ds(at_row, rows_half), pl.ds(at_col, cols_half)] = ref[t]


def store_quarters(grad_ref, acc, rows_half, cols_half):
    for r in range(2):
        for c in range(2):
            for part in range(cols_half // LANES):
                lane = r * cols_half + part * LANES
                grad_ref[r, c, part * rows_half:(part + 1) * rows_half, :] = (
                    acc[c * rows_half:(c + 1) * rows_half, lane:lane + LANES].astype(BF16)
                )


def ffn_kernel(
    place_ref, mid_ref, og_ref, norm_ref, own_ref, side_ref, row_ref, far_ref,
    out_ref, gate_ref, up_ref, down_ref,
    weights, acc,
):
    i = pl.program_id(0)
    rows_half, cols_half = own_ref.shape[1], own_ref.shape[2]

    @pl.when(i == 0)
    def _():
        place_weights(place_ref, (own_ref, side_ref, row_ref, far_ref), weights)
        acc[...] = jnp.zeros(acc.shape, F32)

    middle = mid_ref[...]
    og = og_ref[...]
    scale = lax.rsqrt(jnp.mean(middle * middle, axis=-1, keepdims=True) + EPS)
    normed = (middle * scale * norm_ref[...]).astype(BF16)
    og_t = og.astype(F32).T.astype(BF16)
    chunk = cols_half // 2
    mlp_out = jnp.zeros(middle.shape, F32)
    for c in range(2 * cols_half // chunk):
        at = slice(c * chunk, (c + 1) * chunk)
        gate_pre = dot_nn(normed, weights[0, :, at])
        up_pre = dot_nn(normed, weights[1, :, at])
        hidden_low = dot_nn(og, weights[2, :, at]).astype(BF16).astype(F32)
        squashed = 1.0 / (1.0 + jnp.exp(-gate_pre))
        active = gate_pre * squashed
        hidden = (active * up_pre).astype(BF16)
        gate_ref[:, at] = (hidden_low * up_pre * squashed * (1.0 + gate_pre * (1.0 - squashed))).astype(BF16)
        up_ref[:, at] = (hidden_low * active).astype(BF16)
        mlp_out += dot_nt(hidden, weights[2, :, at])
        acc[:, at] += dot_nn(og_t, hidden)
    out_ref[...] = (middle + mlp_out).astype(BF16)

    @pl.when(i == pl.num_programs(0) - 1)
    def _():
        store_quarters(down_ref, acc, rows_half, cols_half)


def ffn(place, middle, out_grad, norm_two, own, side, across, far):
    tokens, width = middle.shape
    rows_half, cols_half = own.shape[1:]
    hidden = 2 * cols_half
    rows = lambda i: (i, 0)
    whole3 = lambda i: (0, 0, 0)
    once = pl.Buffered(1)
    grad_rows = cols_half // LANES * rows_half
    return pl.pallas_call(
        ffn_kernel,
        grid=(tokens // BLOCK,),
        in_specs=[
            pl.BlockSpec(memory_space=pltpu.SMEM),
            pl.BlockSpec((BLOCK, width), rows),
            pl.BlockSpec((BLOCK, width), rows),
            pl.BlockSpec((1, width), lambda i: (0, 0)),
        ] + [pl.BlockSpec(own.shape, whole3, pipeline_mode=once)] * 4,
        out_specs=[
            pl.BlockSpec((BLOCK, width), rows),
            pl.BlockSpec((BLOCK, hidden), rows),
            pl.BlockSpec((BLOCK, hidden), rows),
            pl.BlockSpec((2, 2, grad_rows, LANES), lambda i: (0, 0, 0, 0), pipeline_mode=once),
        ],
        out_shape=[
            jax.ShapeDtypeStruct((tokens, width), BF16),
            jax.ShapeDtypeStruct((tokens, hidden), BF16),
            jax.ShapeDtypeStruct((tokens, hidden), BF16),
            jax.ShapeDtypeStruct((2, 2, grad_rows, LANES), BF16),
        ],
        scratch_shapes=[
            pltpu.VMEM((3, width, hidden), BF16),
            pltpu.VMEM((width, hidden), F32),
        ],
        cost_estimate=pl.CostEstimate(flops=10 * 10**9, bytes_accessed=18 * 10**6, transcendentals=2 * 10**6),
        name="ffn",
    )(place, middle, out_grad, norm_two, own, side, across, far)


def ffn_back_kernel(
    place_ref, mid_ref, og_ref, att_ref, norm_ref, w_out_ref, own_ref, side_ref, row_ref, far_ref,
    gate_ref, up_ref, sel_ref,
    mg_ref, do_ref, delta_ref, ggate_ref, gup_ref,
    weights, acc2, acc_out, acc_gain,
):
    i = pl.program_id(0)
    rows_half, cols_half = own_ref.shape[1], own_ref.shape[2]

    @pl.when(i == 0)
    def _():
        place_weights(place_ref, (own_ref, side_ref, row_ref, far_ref), weights)
        acc2[...] = jnp.zeros(acc2.shape, F32)
        acc_out[...] = jnp.zeros(acc_out.shape, F32)
        acc_gain[...] = jnp.zeros(acc_gain.shape, F32)

    middle = mid_ref[...]
    width = middle.shape[1]
    gain = norm_ref[...]
    scale = lax.rsqrt(jnp.mean(middle * middle, axis=-1, keepdims=True) + EPS)
    normed_t = (middle * scale * gain).T.astype(BF16)
    chunk = cols_half // 2
    normed_grad = jnp.zeros(middle.shape, F32)
    for c in range(2 * cols_half // chunk):
        at = slice(c * chunk, (c + 1) * chunk)
        gate_low, up_low = gate_ref[:, at], up_ref[:, at]
        normed_grad += dot_nt(gate_low, weights[0, :, at]) + dot_nt(up_low, weights[1, :, at])
        acc2[0, :, at] += dot_nn(normed_t, gate_low)
        acc2[1, :, at] += dot_nn(normed_t, up_low)
    acc_gain[:, :width] += jnp.sum((normed_grad * middle * scale).reshape(BLOCK // 8, 8, width), axis=0)
    weighted = normed_grad * gain
    inner = jnp.sum(weighted * middle, axis=-1, keepdims=True)
    middle_grad = (
        og_ref[...].astype(F32) + scale * weighted
        - middle * (scale * scale * scale) * inner / width
    )
    mg_ref[...] = middle_grad
    middle_low = middle_grad.astype(BF16)
    attended = att_ref[...]
    acc_out[:, :width] += dot_tn(attended, middle_low)
    att_low = dot_nt(middle_low, w_out_ref[...]).astype(BF16)
    for h in range(HEADS):
        do_ref[h] = att_low[:, h * HEAD:(h + 1) * HEAD]
    product = att_low.astype(F32) * attended.astype(F32)
    coarse = product.astype(BF16)
    fine = (product - coarse.astype(F32)).astype(BF16)
    delta_ref[...] = dot_nt(sel_ref[...], coarse) + dot_nt(sel_ref[...], fine)

    @pl.when(i == pl.num_programs(0) - 1)
    def _():
        store_quarters(ggate_ref, acc2.at[0], rows_half, cols_half)
        store_quarters(gup_ref, acc2.at[1], rows_half, cols_half)
        base = cols_half // LANES * rows_half
        quarter = width // 4
        chunks = acc_out.shape[1] // LANES
        for n in range(4):
            for part in range(chunks):
                gup_ref[n // 2, n % 2, base + part * quarter:base + (part + 1) * quarter, :] = (
                    acc_out[n * quarter:(n + 1) * quarter, part * LANES:(part + 1) * LANES].astype(BF16)
                )
        base += chunks * quarter
        extra = gup_ref.shape[2] - base
        for n in range(4):
            gup_ref[n // 2, n % 2, base:, :] = jnp.zeros((extra, LANES), BF16)
        for part in range(chunks):
            gup_ref[0, 0, base + 16 * part:base + 16 * part + 8, :] = acc_gain[:, part * LANES:(part + 1) * LANES].astype(BF16)


def padded_width(width):
    return -(-width // LANES) * LANES


def up_rows(width, grad_rows):
    chunks = padded_width(width) // LANES
    total = grad_rows + chunks * width // 4 + 16 * chunks
    return -(-total // 512) * 512


def ffn_back(place, middle, out_grad, attended, norm_two, w_out, own, side, across, far, gate_low, up_low, selector):
    tokens, width = middle.shape
    rows_half, cols_half = own.shape[1:]
    hidden = 2 * cols_half
    rows = lambda i: (i, 0)
    whole = lambda i: (0, 0)
    once = pl.Buffered(1)
    grad_rows = cols_half // LANES * rows_half
    tall = up_rows(width, grad_rows)
    pair = pl.BlockSpec((2,) + own.shape[1:], lambda i: (0, 0, 0), pipeline_mode=once)
    return pl.pallas_call(
        ffn_back_kernel,
        grid=(tokens // BLOCK,),
        in_specs=[
            pl.BlockSpec(memory_space=pltpu.SMEM),
            pl.BlockSpec((BLOCK, width), rows),
            pl.BlockSpec((BLOCK, width), rows),
            pl.BlockSpec((BLOCK, width), rows),
            pl.BlockSpec((1, width), whole),
            pl.BlockSpec(w_out.shape, whole, pipeline_mode=once),
            pair, pair, pair, pair,
            pl.BlockSpec((BLOCK, hidden), rows),
            pl.BlockSpec((BLOCK, hidden), rows),
            pl.BlockSpec(selector.shape, whole),
        ],
        out_specs=[
            pl.BlockSpec((BLOCK, width), rows),
            pl.BlockSpec((HEADS, BLOCK, HEAD), lambda i: (0, i, 0)),
            pl.BlockSpec((16, BLOCK), lambda i: (0, i)),
            pl.BlockSpec((2, 2, grad_rows, LANES), lambda i: (0,) * 4, pipeline_mode=once),
            pl.BlockSpec((2, 2, tall, LANES), lambda i: (0,) * 4, pipeline_mode=once),
        ],
        out_shape=[
            jax.ShapeDtypeStruct((tokens, width), F32),
            jax.ShapeDtypeStruct((HEADS, tokens, HEAD), BF16),
            jax.ShapeDtypeStruct((16, tokens), F32),
            jax.ShapeDtypeStruct((2, 2, grad_rows, LANES), BF16),
            jax.ShapeDtypeStruct((2, 2, tall, LANES), BF16),
        ],
        scratch_shapes=[
            pltpu.VMEM((2, width, hidden), BF16),
            pltpu.VMEM((2, width, hidden), F32),
            pltpu.VMEM((width, padded_width(width)), F32),
            pltpu.VMEM((8, padded_width(width)), F32),
        ],
        cost_estimate=pl.CostEstimate(flops=9 * 10**9, bytes_accessed=20 * 10**6, transcendentals=10**4),
        name="ffn_back",
    )(place, middle, out_grad, attended, norm_two, w_out, own, side, across, far, gate_low, up_low, selector)


def back_kernel(
    q_ref, k_ref, v_ref, do_ref, lse_ref, delta_ref, start_ref, cos_ref, sin_ref, normed_ref,
    low_ref, grad_ref,
    dq_all, dk, dv, acc,
    *, group,
):
    j = pl.program_id(0)
    blocks = pl.num_programs(0)

    @pl.when(j == 0)
    def _():
        dq_all[...] = jnp.zeros(dq_all.shape, F32)
        acc[...] = jnp.zeros(acc.shape, F32)

    dk[...] = jnp.zeros(dk.shape, F32)
    dv[...] = jnp.zeros(dv.shape, F32)
    keys, values = k_ref[0], v_ref[0]
    keys_t = keys.astype(F32).T.astype(BF16)

    def tile(i, diagonal):
        span = pl.ds(pl.multiple_of(i * BLOCK, BLOCK), BLOCK)
        start_row = start_ref[:, span]
        mask = allowed_tile(start_row, j * BLOCK, i * BLOCK, diagonal)
        for h in range(GROUP):
            head = group * GROUP + h
            queries, grads = q_ref[h, span, :], do_ref[h, span, :]
            raw = dot_nt(keys, queries) * LOG2E - lse_ref[head:head + 1, span]
            soft = jnp.where(mask, jnp.exp2(raw), 0.0)
            prob_grad = dot_nt(values, grads)
            score_low = (soft * (prob_grad - delta_ref[head:head + 1, span])).astype(BF16)
            dv[...] += dot_nn(soft.astype(BF16), grads)
            dk[...] += dot_nn(score_low, queries)
            dq_all[i, h] += dot_nn(keys_t, score_low)

    def step(i, carry):
        tile(i, False)
        return carry

    tile(j, True)
    lax.fori_loop(j + 1, blocks, step, 0)

    cosine, sine = cos_ref[...], sin_ref[...]
    query_grad = jnp.concatenate([dq_all[j, h] for h in range(GROUP)], axis=0).T * (HEAD ** -0.5)
    turned = jnp.concatenate([query_grad, dk[...]], axis=1)
    columns = []
    for c in range(turned.shape[1] // LANES):
        part = turned[:, c * LANES:(c + 1) * LANES]
        columns.append((part * cosine - partner_lanes(part) * sine).astype(BF16))
    low = jnp.concatenate(columns + [dv[...].astype(BF16)], axis=1)
    low_ref[...] = low
    acc[...] += dot_tn(normed_ref[...], low)

    @pl.when(j == blocks - 1)
    def _():
        grad_ref[...] = acc[...].astype(BF16)


def back(group, q, k, v, do, lse, delta, start, cosine, sine, normed):
    tokens, width = normed.shape
    blocks = tokens // BLOCK
    size = (GROUP + 2) * HEAD
    rows = lambda j: (j, 0)
    whole = lambda j: (0, 0)
    group3 = lambda j: (group, 0, 0)
    mine3 = lambda j: (group, j, 0)
    return pl.pallas_call(
        functools.partial(back_kernel, group=group),
        grid=(blocks,),
        in_specs=[
            pl.BlockSpec((GROUP, tokens, HEAD), group3),
            pl.BlockSpec((1, BLOCK, HEAD), mine3),
            pl.BlockSpec((1, BLOCK, HEAD), mine3),
            pl.BlockSpec((GROUP, tokens, HEAD), group3),
            pl.BlockSpec(lse.shape, whole),
            pl.BlockSpec(delta.shape, whole),
            pl.BlockSpec(start.shape, whole),
            pl.BlockSpec((BLOCK, LANES), rows),
            pl.BlockSpec((BLOCK, LANES), rows),
            pl.BlockSpec((BLOCK, width), rows),
        ],
        out_specs=[
            pl.BlockSpec((BLOCK, size), rows),
            pl.BlockSpec((width, size), whole),
        ],
        out_shape=[
            jax.ShapeDtypeStruct((tokens, size), BF16),
            jax.ShapeDtypeStruct((width, size), BF16),
        ],
        scratch_shapes=[
            pltpu.VMEM((blocks, GROUP, HEAD, BLOCK), F32),
            pltpu.VMEM((BLOCK, HEAD), F32),
            pltpu.VMEM((BLOCK, HEAD), F32),
            pltpu.VMEM((width, size), F32),
        ],
        cost_estimate=pl.CostEstimate(flops=3 * 10**9, bytes_accessed=6 * 10**6, transcendentals=2 * 10**6),
    )(q, k, v, do, lse, delta, start, cosine, sine, normed)


def input_kernel(low0_ref, low1_ref, low2_ref, w_qkv_ref, inputs_ref, mg_ref, norm_ref, ig_ref, gain_ref, w_all):
    j = pl.program_id(0)
    size = GROUP * HEAD

    @pl.when(j == 0)
    def _():
        gain_ref[...] = jnp.zeros(gain_ref.shape, F32)
        weights = w_qkv_ref[...]
        for g in range(KV_HEADS):
            key_at = HEADS * HEAD + g * HEAD
            value_at = key_at + KV_HEADS * HEAD
            w_all[g] = jnp.concatenate(
                [weights[:, g * size:(g + 1) * size], weights[:, key_at:key_at + HEAD], weights[:, value_at:value_at + HEAD]],
                axis=1,
            )

    normed_grad = dot_nt(low0_ref[...], w_all[0]) + dot_nt(low1_ref[...], w_all[1]) + dot_nt(low2_ref[...], w_all[2])
    x = inputs_ref[...].astype(F32)
    gain = norm_ref[...]
    scale = lax.rsqrt(jnp.mean(x * x, axis=-1, keepdims=True) + EPS)
    gain_ref[...] += jnp.sum((normed_grad * x * scale).reshape(BLOCK // 8, 8, x.shape[1]), axis=0)
    weighted = normed_grad * gain
    inner = jnp.sum(weighted * x, axis=-1, keepdims=True)
    ig_ref[...] = mg_ref[...] + scale * weighted - x * (scale * scale * scale) * inner / x.shape[1]


def input_back(lows, w_qkv, inputs, middle_grad, norm_one):
    tokens, width = inputs.shape
    size = lows[0].shape[1]
    rows = lambda j: (j, 0)
    whole = lambda j: (0, 0)
    low_spec = pl.BlockSpec((BLOCK, size), rows)
    return pl.pallas_call(
        input_kernel,
        grid=(tokens // BLOCK,),
        in_specs=[
            low_spec, low_spec, low_spec,
            pl.BlockSpec(w_qkv.shape, whole),
            pl.BlockSpec((BLOCK, width), rows),
            pl.BlockSpec((BLOCK, width), rows),
            pl.BlockSpec((1, width), whole),
        ],
        out_specs=[pl.BlockSpec((BLOCK, width), rows), pl.BlockSpec((8, width), whole)],
        out_shape=[jax.ShapeDtypeStruct((tokens, width), F32), jax.ShapeDtypeStruct((8, width), F32)],
        scratch_shapes=[pltpu.VMEM((KV_HEADS, width, size), BF16)],
        cost_estimate=pl.CostEstimate(flops=12 * 10**8, bytes_accessed=9 * 10**6, transcendentals=10**4),
        name="input_back",
    )(*lows, w_qkv, inputs, middle_grad, norm_one)


def places(seq_ids):
    position = jnp.arange(seq_ids.shape[0], dtype=jnp.int32)
    previous = jnp.concatenate([seq_ids[:1] - 1, seq_ids[:-1]])
    start = lax.cummax(jnp.where(seq_ids != previous, position, 0), axis=0)
    return start, (position - start).astype(F32)


def tables(place):
    half = HEAD // 2
    frequency = THETA ** (-2.0 * jnp.arange(half, dtype=F32) / HEAD)
    angles = frequency[:, None] * place[None, :]
    cosine, sine = jnp.cos(angles).T, jnp.sin(angles).T
    copies = LANES // HEAD
    return (
        jnp.concatenate([cosine, cosine] * copies, axis=1),
        jnp.concatenate([-sine, sine] * copies, axis=1),
    )


def bits(size):
    out, bit = [], 1
    while bit < size:
        out.append(bit)
        bit *= 2
    return out


def swap_with(data, axis, bit):
    size = lax.axis_size(axis)
    return lax.ppermute(data, axis, [(n, n ^ bit) for n in range(size)])


def own_bit(axis, bit):
    return (lax.axis_index(axis) // bit) % 2


def halve(data, dim, axis, bit):
    mine = own_bit(axis, bit)
    shape = data.shape
    halves = data.reshape(shape[:dim] + (2, shape[dim] // 2) + shape[dim + 1:])
    sent = lax.dynamic_index_in_dim(halves, 1 - mine, dim, keepdims=False)
    kept = lax.dynamic_index_in_dim(halves, mine, dim, keepdims=False)
    arrived = swap_with(sent, axis, bit)
    return (kept.astype(F32) + arrived.astype(F32)).astype(BF16)


def double(data, axis, bit):
    lower = own_bit(axis, bit) == 0
    arrived = swap_with(data, axis, bit)
    return jnp.concatenate([jnp.where(lower, data, arrived), jnp.where(lower, arrived, data)], axis=0)


def swap_add(data, axis, bit):
    arrived = swap_with(data, axis, bit)
    return (data.astype(F32) + arrived.astype(F32)).astype(BF16)


def reduce_blocks(data, order):
    data = halve(data.reshape((2,) + data.shape[1:]), 0, "row", 1)[0]
    for axis, bit in order:
        dim = 0 if axis == "col" else 1
        data = halve(data, dim, axis, bit)
    data = data.reshape(data.shape[-2:])
    for axis, bit in reversed(order):
        if axis != "col":
            data = double(data, axis, bit)
    return data


def layer(inputs, seq_ids, norm_one, w_qkv, w_out, norm_two, w_gate, w_up, w_down, out_grad):
    dp_bits = [("dp", bit) for bit in bits(lax.axis_size("dp"))]
    col = [("col", 1)]
    width = inputs.shape[1]
    own = jnp.stack([w_gate, w_up, w_down.T])
    side = swap_with(own, "col", 1)
    across = swap_with(own, "row", 1)
    start, place = places(seq_ids)
    start = start[None, :]
    cosine, sine = tables(place)
    gain_one, gain_two = norm_one[None, :], norm_two[None, :]
    q, k, v, lse, attended, middle, normed = front(inputs, start, cosine, sine, gain_one, w_qkv, w_out)
    far = swap_with(side, "row", 1)
    selector = (jnp.arange(16)[:, None] == jnp.arange(width)[None, :] // HEAD).astype(BF16)
    spot = jnp.stack([lax.axis_index("col"), lax.axis_index("row")]).astype(jnp.int32)
    outputs, gate_low, up_low, down = ffn(spot, middle, out_grad, gain_two, own, side, across, far)
    middle_grad, do, delta, gate, up = ffn_back(
        spot, middle, out_grad, attended, gain_two, w_out, own, side, across, far, gate_low, up_low, selector
    )
    lows, slices = [], []
    for g in range(KV_HEADS):
        low, part = back(g, q, k, v, do, lse, delta, start, cosine, sine, normed)
        lows.append(low)
        slices.append(part)
    input_grad, gain_one_part = input_back(lows, w_qkv, inputs, middle_grad, gain_one)

    down = reduce_blocks(down, col + dp_bits)
    gate = reduce_blocks(gate, col + dp_bits)
    up = reduce_blocks(up, dp_bits[1:] + dp_bits[:1] + col)
    grad_rows = down.shape[0]
    rest = double(up[grad_rows:], "col", 1)
    rest = double(rest, "row", 1).reshape(4, -1, LANES)

    def total(data):
        rows = data.shape[0]
        data = halve(data.reshape(2, rows // 2, LANES), 0, "row", 1)[0]
        for axis, bit in col + dp_bits:
            data = swap_add(data, axis, bit)
        return double(data, "row", 1)

    def tall(block):
        block = jnp.pad(block, ((0, 0), (0, padded_width(block.shape[1]) - block.shape[1])))
        return jnp.concatenate([block[:, at:at + LANES] for at in range(0, block.shape[1], LANES)], axis=0)

    def flat(block, rows):
        return jnp.concatenate([block[at:at + rows] for at in range(0, block.shape[0], rows)], axis=1)

    first = total(jnp.concatenate([tall(slices[0]), tall(slices[1])], axis=0))
    gain_rows = tall(gain_one_part.astype(BF16))
    last = tall(slices[2])
    size = slices[0].shape[1]
    cut = last.shape[0]
    last = total(jnp.concatenate([last, gain_rows], axis=0))
    groups = [flat(first[:cut], width)[:, :size], flat(first[cut:], width)[:, :size], flat(last[:cut], width)[:, :size]]
    lead = GROUP * HEAD
    grad_qkv = jnp.concatenate(
        [g[:, :lead] for g in groups] + [g[:, lead:lead + HEAD] for g in groups] + [g[:, lead + HEAD:] for g in groups], axis=1
    ).astype(F32)
    grad_norm_one = jnp.sum(flat(last[cut:], 8)[:, :width].astype(F32), axis=0)
    chunks = padded_width(width) // LANES
    quarter = width // 4
    grad_out = jnp.concatenate(
        [flat(rest[n, :chunks * quarter], quarter)[:, :width] for n in range(4)], axis=0
    ).astype(F32)
    base = chunks * quarter
    gain_two_rows = rest[0, base:base + 16 * chunks]
    grad_norm_two = jnp.sum(flat(gain_two_rows, 16)[:8, :width].astype(F32), axis=0)

    def spread(data):
        return data[:grad_rows].reshape(-1, w_gate.shape[0], LANES).astype(F32)

    grad_gate = spread(gate).transpose(1, 0, 2).reshape(w_gate.shape)
    grad_up = spread(up).transpose(1, 0, 2).reshape(w_up.shape)
    grad_down = spread(down).transpose(0, 2, 1).reshape(w_down.shape)
    return (outputs, input_grad, grad_norm_one, grad_qkv, grad_out, grad_norm_two, grad_gate, grad_up, grad_down)


def solution(mesh):
    tokens = P(("dp", "row", "col"), None)
    grid, turned = P("col", "row"), P("row", "col")
    return jax.shard_map(
        layer,
        mesh=mesh,
        in_specs=(tokens, P(("dp", "row", "col")), P(), P(), P(), P(), grid, grid, turned, tokens),
        out_specs=(tokens, tokens, P(), P(), P(), P(), grid, grid, turned),
        check_vma=False,
    )
```

```python
import jax
import jax.numpy as jnp
from jax import lax
from jax.experimental import pallas as pl
from jax.experimental.pallas import tpu as pltpu
from jax.sharding import PartitionSpec as P


HEADS = 9
KV_HEADS = 3
GROUP = HEADS // KV_HEADS
HEAD = 64
BLOCK = 256
LANES = 128
LOG2E = 1.4426950408889634
EPS = 1e-05
THETA = 100000.0
NEG = -1e30
F32 = jnp.float32
BF16 = jnp.bfloat16


def dot_nn(a, b):
    return lax.dot_general(a, b, (((1,), (0,)), ((), ())), preferred_element_type=F32)


def dot_nt(a, b):
    return lax.dot_general(a, b, (((1,), (1,)), ((), ())), preferred_element_type=F32)


def dot_tn(a, b):
    return lax.dot_general(a, b, (((0,), (0,)), ((), ())), preferred_element_type=F32)


def partner_lanes(x):
    lane = lax.broadcasted_iota(jnp.int32, x.shape, 1)
    front = lax.rem(lane, HEAD) < HEAD // 2
    return jnp.where(
        front, pltpu.roll(x, LANES - HEAD // 2, 1), pltpu.roll(x, HEAD // 2, 1)
    )


def allowed_tile(start_row, key_start, query_start, diagonal):
    shape = (BLOCK, start_row.shape[1])
    keys = key_start + lax.broadcasted_iota(jnp.int32, shape, 0)
    mask = keys >= start_row
    if diagonal:
        rows = query_start + lax.rem(lax.broadcasted_iota(jnp.int32, shape, 1), BLOCK)
        mask = mask & (keys <= rows)
    return mask


def front_kernel(
    inputs_ref, start_ref, cos_ref, sin_ref, norm_ref, w_qkv_ref, w_out_ref,
    q_ref, k_ref, v_ref, lse_ref, att_ref, mid_ref,
    k_all, vt_all, acc, stat_m, stat_l,
):
    i = pl.program_id(0)
    x = inputs_ref[...].astype(F32)
    scale = lax.rsqrt(jnp.mean(x * x, axis=-1, keepdims=True) + EPS)
    normed = (x * scale * norm_ref[...]).astype(BF16)
    joined = dot_nn(normed, w_qkv_ref[...])
    width = (HEADS + KV_HEADS) * HEAD
    cosine, sine = cos_ref[...], sin_ref[...]
    for c in range(width // LANES):
        part = joined[:, c * LANES:(c + 1) * LANES]
        turned = (part * cosine + partner_lanes(part) * sine).astype(BF16)
        for half in range(2):
            h = 2 * c + half
            piece = turned[:, half * HEAD:(half + 1) * HEAD]
            if h < HEADS:
                q_ref[h] = piece * BF16(HEAD ** -0.5)
            else:
                k_ref[h - HEADS] = piece
                k_all[h - HEADS, pl.ds(pl.multiple_of(i * BLOCK, BLOCK), BLOCK), :] = piece
    values = joined[:, width:]
    values_t = values.T.astype(BF16)
    for g in range(KV_HEADS):
        v_ref[g] = values[:, g * HEAD:(g + 1) * HEAD].astype(BF16)
        vt_all[g, i] = values_t[g * HEAD:(g + 1) * HEAD, :]
    start = start_ref[...]
    start_row = jnp.concatenate([start] * GROUP, axis=1)
    stat_m[...] = jnp.full(stat_m.shape, NEG, F32)
    stat_l[...] = jnp.zeros(stat_l.shape, F32)
    acc[...] = jnp.zeros(acc.shape, F32)

    def tile(j, diagonal):
        mask = allowed_tile(start_row, j * BLOCK, i * BLOCK, diagonal)
        for g in range(KV_HEADS):
            queries = q_ref[g * GROUP:(g + 1) * GROUP].reshape(GROUP * BLOCK, HEAD)
            keys = k_all[g, pl.ds(pl.multiple_of(j * BLOCK, BLOCK), BLOCK), :]
            scores = jnp.where(mask, dot_nt(keys, queries) * LOG2E, NEG)
            peak_old = stat_m[g:g + 1]
            peak = jnp.maximum(peak_old, jnp.max(scores, axis=0, keepdims=True))
            expo = jnp.exp2(scores - peak)
            expo = jnp.where(mask, expo, 0.0)
            fade = jnp.exp2(peak_old - peak)
            stat_m[g:g + 1] = peak
            stat_l[g:g + 1] = stat_l[g:g + 1] * fade + jnp.sum(expo, axis=0, keepdims=True)
            acc[g] = acc[g] * fade + dot_nn(vt_all[g, j], expo.astype(BF16))

    def step(j, carry):
        tile(j, False)
        return carry

    lax.fori_loop(0, i, step, 0)
    tile(i, True)
    pieces = []
    for g in range(KV_HEADS):
        total = stat_l[g:g + 1]
        mixed = acc[g] / total
        logsum = stat_m[g:g + 1] + jnp.log2(total)
        for h in range(GROUP):
            lse_ref[g * GROUP + h:g * GROUP + h + 1, :] = logsum[:, h * BLOCK:(h + 1) * BLOCK]
            pieces.append(mixed[:, h * BLOCK:(h + 1) * BLOCK])
    attended = jnp.concatenate(pieces, axis=0).T.astype(BF16)
    att_ref[...] = attended
    mid_ref[...] = x + dot_nn(attended, w_out_ref[...])


def front(inputs, start, cosine, sine, norm_one, w_qkv, w_out):
    tokens, width = inputs.shape
    blocks = tokens // BLOCK
    whole = lambda i: (0, 0)
    rows = lambda i: (i, 0)
    return pl.pallas_call(
        front_kernel,
        grid=(blocks,),
        in_specs=[
            pl.BlockSpec((BLOCK, width), rows),
            pl.BlockSpec((1, BLOCK), lambda i: (0, i)),
            pl.BlockSpec((BLOCK, LANES), rows),
            pl.BlockSpec((BLOCK, LANES), rows),
            pl.BlockSpec((1, width), whole),
            pl.BlockSpec(w_qkv.shape, whole),
            pl.BlockSpec(w_out.shape, whole),
        ],
        out_specs=[
            pl.BlockSpec((HEADS, BLOCK, HEAD), lambda i: (0, i, 0)),
            pl.BlockSpec((KV_HEADS, BLOCK, HEAD), lambda i: (0, i, 0)),
            pl.BlockSpec((KV_HEADS, BLOCK, HEAD), lambda i: (0, i, 0)),
            pl.BlockSpec((16, BLOCK), lambda i: (0, i)),
            pl.BlockSpec((BLOCK, width), rows),
            pl.BlockSpec((BLOCK, width), rows),
        ],
        out_shape=[
            jax.ShapeDtypeStruct((HEADS, tokens, HEAD), BF16),
            jax.ShapeDtypeStruct((KV_HEADS, tokens, HEAD), BF16),
            jax.ShapeDtypeStruct((KV_HEADS, tokens, HEAD), BF16),
            jax.ShapeDtypeStruct((16, tokens), F32),
            jax.ShapeDtypeStruct((tokens, width), BF16),
            jax.ShapeDtypeStruct((tokens, width), F32),
        ],
        scratch_shapes=[
            pltpu.VMEM((KV_HEADS, tokens, HEAD), BF16),
            pltpu.VMEM((KV_HEADS, blocks, HEAD, BLOCK), BF16),
            pltpu.VMEM((KV_HEADS, HEAD, GROUP * BLOCK), F32),
            pltpu.VMEM((8, GROUP * BLOCK), F32),
            pltpu.VMEM((8, GROUP * BLOCK), F32),
        ],
        cost_estimate=pl.CostEstimate(flops=6 * 10**9, bytes_accessed=12 * 10**6, transcendentals=6 * 10**6),
        name="front",
    )(inputs, start, cosine, sine, norm_one, w_qkv, w_out)


def mlp_kernel(
    place_ref, mid_ref, og_ref, att_ref, norm_ref, w_out_ref, own_ref, side_ref, row_ref, far_ref, sel_ref,
    out_ref, mg_ref, do_ref, delta_ref, g00_ref, g01_ref, g10_ref, g11_ref,
    weights, acc3, acc_out, acc_gain,
):
    i = pl.program_id(0)
    rows_half, cols_half = own_ref.shape[1], own_ref.shape[2]
    col, row = place_ref[0], place_ref[1]

    @pl.when(i == 0)
    def _():
        for ref, c, r in ((own_ref, col, row), (side_ref, 1 - col, row), (row_ref, col, 1 - row), (far_ref, 1 - col, 1 - row)):
            at_row = pl.multiple_of(c * rows_half, 32)
            at_col = pl.multiple_of(r * cols_half, LANES)
            for t in range(3):
                weights[t, pl.ds(at_row, rows_half), pl.ds(at_col, cols_half)] = ref[t]
        acc3[...] = jnp.zeros(acc3.shape, F32)
        acc_out[...] = jnp.zeros(acc_out.shape, F32)
        acc_gain[...] = jnp.zeros(acc_gain.shape, F32)

    middle = mid_ref[...]
    og = og_ref[...]
    gain = norm_ref[...]
    scale = lax.rsqrt(jnp.mean(middle * middle, axis=-1, keepdims=True) + EPS)
    normed = (middle * scale * gain).astype(BF16)
    og_t = og.astype(F32).T.astype(BF16)
    normed_t = normed.astype(F32).T.astype(BF16)
    chunk = cols_half // 2
    mlp_out = jnp.zeros(middle.shape, F32)
    normed_grad = jnp.zeros(middle.shape, F32)
    for c in range(2 * cols_half // chunk):
        at = slice(c * chunk, (c + 1) * chunk)
        gate_pre = dot_nn(normed, weights[0, :, at])
        up_pre = dot_nn(normed, weights[1, :, at])
        hidden_low = dot_nn(og, weights[2, :, at]).astype(BF16).astype(F32)
        squashed = 1.0 / (1.0 + jnp.exp(-gate_pre))
        active = gate_pre * squashed
        hidden = (active * up_pre).astype(BF16)
        gate_low = (hidden_low * up_pre * squashed * (1.0 + gate_pre * (1.0 - squashed))).astype(BF16)
        up_low = (hidden_low * active).astype(BF16)
        mlp_out += dot_nt(hidden, weights[2, :, at])
        normed_grad += dot_nt(gate_low, weights[0, :, at]) + dot_nt(up_low, weights[1, :, at])
        acc3[0, :, at] += dot_nn(normed_t, gate_low)
        acc3[1, :, at] += dot_nn(normed_t, up_low)
        acc3[2, :, at] += dot_nn(og_t, hidden)
    out_ref[...] = (middle + mlp_out).astype(BF16)
    width = middle.shape[1]
    acc_gain[:, :width] += jnp.sum((normed_grad * middle * scale).reshape(BLOCK // 8, 8, width), axis=0)
    weighted = normed_grad * gain
    inner = jnp.sum(weighted * middle, axis=-1, keepdims=True)
    middle_grad = (
        og.astype(F32) + scale * weighted
        - middle * (scale * scale * scale) * inner / middle.shape[1]
    )
    mg_ref[...] = middle_grad
    middle_low = middle_grad.astype(BF16)
    attended = att_ref[...]
    acc_out[:, :width] += dot_tn(attended, middle_low)
    att_low = dot_nt(middle_low, w_out_ref[...]).astype(BF16)
    for h in range(HEADS):
        do_ref[h] = att_low[:, h * HEAD:(h + 1) * HEAD]
    product = att_low.astype(F32) * attended.astype(F32)
    coarse = product.astype(BF16)
    fine = (product - coarse.astype(F32)).astype(BF16)
    delta_ref[...] = dot_nt(sel_ref[...], coarse) + dot_nt(sel_ref[...], fine)

    @pl.when(i == pl.num_programs(0) - 1)
    def _():
        quarter = width // 4
        chunks = acc_out.shape[1] // LANES
        for ref, c, r in ((g00_ref, col, row), (g01_ref, 1 - col, row), (g10_ref, col, 1 - row), (g11_ref, 1 - col, 1 - row)):
            at_row = pl.multiple_of(c * rows_half, 32)
            base = 0
            for t in range(3):
                for part in range(cols_half // LANES):
                    lane = pl.ds(pl.multiple_of(r * cols_half + part * LANES, LANES), LANES)
                    ref[base:base + rows_half, :] = acc3[t, pl.ds(at_row, rows_half), lane].astype(BF16)
                    base += rows_half
            at_row = pl.multiple_of((2 * r + c) * quarter, 16)
            for part in range(chunks):
                at = slice(part * LANES, (part + 1) * LANES)
                ref[base:base + quarter, :] = acc_out[pl.ds(at_row, quarter), at].astype(BF16)
                base += quarter
            share = jnp.where((r == 0) & (c == 0), 1.0, 0.0)
            for part in range(chunks):
                at = slice(part * LANES, (part + 1) * LANES)
                gains = acc_gain[:, at] * share
                ref[base:base + 16, :] = jnp.concatenate([gains, jnp.zeros_like(gains)], axis=0).astype(BF16)
                base += 16
            ref[base:, :] = jnp.zeros((ref.shape[0] - base, LANES), BF16)


def padded_width(width):
    return -(-width // LANES) * LANES


def round_up(count, unit):
    return -(-count // unit) * unit


def mlp(unit, place, middle, out_grad, attended, norm_two, w_out, own, side, across, far, selector):
    tokens, width = middle.shape
    rows_half, cols_half = own.shape[1:]
    blocks = tokens // BLOCK
    chunks = padded_width(width) // LANES
    tall = round_up(3 * cols_half // LANES * rows_half + chunks * (width // 4 + 16), unit)
    block = pl.BlockSpec((tall, LANES), lambda i: (0, 0), pipeline_mode=pl.Buffered(1))
    rows = lambda i: (i, 0)
    whole = lambda i: (0, 0)
    whole3 = lambda i: (0, 0, 0)
    once = pl.Buffered(1)
    return pl.pallas_call(
        mlp_kernel,
        grid=(blocks,),
        in_specs=[
            pl.BlockSpec(memory_space=pltpu.SMEM),
            pl.BlockSpec((BLOCK, width), rows),
            pl.BlockSpec((BLOCK, width), rows),
            pl.BlockSpec((BLOCK, width), rows),
            pl.BlockSpec((1, width), whole),
            pl.BlockSpec(w_out.shape, whole, pipeline_mode=once),
            pl.BlockSpec(own.shape, whole3, pipeline_mode=once),
            pl.BlockSpec(own.shape, whole3, pipeline_mode=once),
            pl.BlockSpec(own.shape, whole3, pipeline_mode=once),
            pl.BlockSpec(own.shape, whole3, pipeline_mode=once),
            pl.BlockSpec(selector.shape, whole),
        ],
        out_specs=[
            pl.BlockSpec((BLOCK, width), rows),
            pl.BlockSpec((BLOCK, width), rows),
            pl.BlockSpec((HEADS, BLOCK, HEAD), lambda i: (0, i, 0)),
            pl.BlockSpec((16, BLOCK), lambda i: (0, i)),
            block, block, block, block,
        ],
        out_shape=[
            jax.ShapeDtypeStruct((tokens, width), BF16),
            jax.ShapeDtypeStruct((tokens, width), F32),
            jax.ShapeDtypeStruct((HEADS, tokens, HEAD), BF16),
            jax.ShapeDtypeStruct((16, tokens), F32),
        ] + [jax.ShapeDtypeStruct((tall, LANES), BF16)] * 4,
        scratch_shapes=[
            pltpu.VMEM((3, 2 * rows_half, 2 * cols_half), BF16),
            pltpu.VMEM((3, 2 * rows_half, 2 * cols_half), F32),
            pltpu.VMEM((width, padded_width(width)), F32),
            pltpu.VMEM((8, padded_width(width)), F32),
        ],
        cost_estimate=pl.CostEstimate(flops=18 * 10**9, bytes_accessed=24 * 10**6, transcendentals=2 * 10**6),
        name="mlp",
    )(place, middle, out_grad, attended, norm_two, w_out, own, side, across, far, selector)


def back_kernel(
    place_ref, q_ref, k_ref, v_ref, do_ref, lse_ref, delta_ref, start_ref, cos_ref, sin_ref,
    inputs_ref, mg_ref, norm_ref, w_qkv_ref,
    ig_ref, keep_ref, send_ref,
    dq_all, dk, dv, acc_qkv, acc_gain,
):
    j = pl.program_id(0)
    blocks = pl.num_programs(0)

    @pl.when(j == 0)
    def _():
        dq_all[...] = jnp.zeros(dq_all.shape, F32)
        acc_qkv[...] = jnp.zeros(acc_qkv.shape, F32)
        acc_gain[...] = jnp.zeros(acc_gain.shape, F32)

    dk[...] = jnp.zeros(dk.shape, F32)
    dv[...] = jnp.zeros(dv.shape, F32)
    keys_t = [k_ref[g].astype(F32).T.astype(BF16) for g in range(KV_HEADS)]

    def tile(i, diagonal):
        at = pl.multiple_of(i * BLOCK, BLOCK)
        span = pl.ds(at, BLOCK)
        start_row = jnp.concatenate([start_ref[:, span]] * GROUP, axis=1)
        mask = allowed_tile(start_row, j * BLOCK, i * BLOCK, diagonal)
        for g in range(KV_HEADS):
            heads = range(g * GROUP, (g + 1) * GROUP)
            queries = q_ref[g * GROUP:(g + 1) * GROUP, span, :].reshape(GROUP * BLOCK, HEAD)
            grads = do_ref[g * GROUP:(g + 1) * GROUP, span, :].reshape(GROUP * BLOCK, HEAD)
            lse_row = jnp.concatenate([lse_ref[h:h + 1, span] for h in heads], axis=1)
            delta_row = jnp.concatenate([delta_ref[h:h + 1, span] for h in heads], axis=1)
            keys, values = k_ref[g], v_ref[g]
            soft = jnp.where(mask, jnp.exp2(dot_nt(keys, queries) * LOG2E - lse_row), 0.0)
            prob_grad = dot_nt(values, grads)
            score_low = (soft * (prob_grad - delta_row)).astype(BF16)
            dv[g] += dot_nn(soft.astype(BF16), grads)
            dk[g] += dot_nn(score_low, queries)
            dq_all[i, g] += dot_nn(keys_t[g], score_low)

    def step(i, carry):
        tile(i, False)
        return carry

    tile(j, True)
    lax.fori_loop(j + 1, blocks, step, 0)

    cosine, sine = cos_ref[...], sin_ref[...]
    pieces = []
    for g in range(KV_HEADS):
        part = dq_all[j, g] * (HEAD ** -0.5)
        pieces += [part[:, h * BLOCK:(h + 1) * BLOCK] for h in range(GROUP)]
    query_grad = jnp.concatenate(pieces, axis=0).T
    turned = jnp.concatenate([query_grad, dk[0], dk[1], dk[2]], axis=1)
    columns = []
    for c in range(turned.shape[1] // LANES):
        part = turned[:, c * LANES:(c + 1) * LANES]
        columns.append((part * cosine - partner_lanes(part) * sine).astype(BF16))
    values_low = jnp.concatenate([dv[0], dv[1], dv[2]], axis=1).astype(BF16)
    joined_low = jnp.concatenate(columns + [values_low], axis=1)

    x = inputs_ref[...].astype(F32)
    gain = norm_ref[...]
    scale = lax.rsqrt(jnp.mean(x * x, axis=-1, keepdims=True) + EPS)
    normed = (x * scale * gain).astype(BF16)
    acc_qkv[:, :joined_low.shape[1]] += dot_tn(normed, joined_low)
    normed_grad = dot_nt(joined_low, w_qkv_ref[...])
    acc_gain[:, :x.shape[1]] += jnp.sum((normed_grad * x * scale).reshape(BLOCK // 8, 8, x.shape[1]), axis=0)
    weighted = normed_grad * gain
    inner = jnp.sum(weighted * x, axis=-1, keepdims=True)
    ig_ref[...] = mg_ref[...] + scale * weighted - x * (scale * scale * scale) * inner / x.shape[1]

    @pl.when(j == blocks - 1)
    def _():
        row = place_ref[1]
        width = x.shape[1]
        half = acc_qkv.shape[1] // 2
        for ref, r in ((keep_ref, row), (send_ref, 1 - row)):
            base = 0
            for part in range(half // LANES):
                lane = pl.ds(pl.multiple_of(r * half + part * LANES, LANES), LANES)
                ref[base:base + width, :] = acc_qkv[:, lane].astype(BF16)
                base += width
            share = jnp.where(r == 0, 1.0, 0.0)
            for part in range(acc_gain.shape[1] // LANES):
                gains = acc_gain[:, part * LANES:(part + 1) * LANES] * share
                ref[base:base + 16, :] = jnp.concatenate([gains, jnp.zeros_like(gains)], axis=0).astype(BF16)
                base += 16
            ref[base:, :] = jnp.zeros((ref.shape[0] - base, LANES), BF16)


def back(unit, place, q, k, v, do, lse, delta, start, cosine, sine, inputs, middle_grad, norm_one, w_qkv):
    tokens, width = inputs.shape
    blocks = tokens // BLOCK
    rows = lambda j: (j, 0)
    whole = lambda j: (0, 0)
    whole3 = lambda j: (0, 0, 0)
    mine3 = lambda j: (0, j, 0)
    wide = round_up(w_qkv.shape[1], 2 * LANES)
    tall = round_up(wide // 2 // LANES * width + 16 * padded_width(width) // LANES, unit)
    block = pl.BlockSpec((tall, LANES), whole)
    return pl.pallas_call(
        back_kernel,
        grid=(blocks,),
        in_specs=[
            pl.BlockSpec(memory_space=pltpu.SMEM),
            pl.BlockSpec(q.shape, whole3),
            pl.BlockSpec((KV_HEADS, BLOCK, HEAD), mine3),
            pl.BlockSpec((KV_HEADS, BLOCK, HEAD), mine3),
            pl.BlockSpec(do.shape, whole3),
            pl.BlockSpec(lse.shape, whole),
            pl.BlockSpec(delta.shape, whole),
            pl.BlockSpec(start.shape, whole),
            pl.BlockSpec((BLOCK, LANES), rows),
            pl.BlockSpec((BLOCK, LANES), rows),
            pl.BlockSpec((BLOCK, width), rows),
            pl.BlockSpec((BLOCK, width), rows),
            pl.BlockSpec((1, width), whole),
            pl.BlockSpec(w_qkv.shape, whole),
        ],
        out_specs=[
            pl.BlockSpec((BLOCK, width), rows),
            block, block,
        ],
        out_shape=[
            jax.ShapeDtypeStruct((tokens, width), F32),
            jax.ShapeDtypeStruct((tall, LANES), BF16),
            jax.ShapeDtypeStruct((tall, LANES), BF16),
        ],
        scratch_shapes=[
            pltpu.VMEM((blocks, KV_HEADS, HEAD, GROUP * BLOCK), F32),
            pltpu.VMEM((KV_HEADS, BLOCK, HEAD), F32),
            pltpu.VMEM((KV_HEADS, BLOCK, HEAD), F32),
            pltpu.VMEM((width, wide), F32),
            pltpu.VMEM((8, padded_width(width)), F32),
        ],
        cost_estimate=pl.CostEstimate(flops=8 * 10**9, bytes_accessed=16 * 10**6, transcendentals=6 * 10**6),
        name="back",
    )(place, q, k, v, do, lse, delta, start, cosine, sine, inputs, middle_grad, norm_one, w_qkv)


def places(seq_ids):
    position = jnp.arange(seq_ids.shape[0], dtype=jnp.int32)
    previous = jnp.concatenate([seq_ids[:1] - 1, seq_ids[:-1]])
    start = lax.cummax(jnp.where(seq_ids != previous, position, 0), axis=0)
    return start, (position - start).astype(F32)


def tables(place):
    half = HEAD // 2
    frequency = THETA ** (-2.0 * jnp.arange(half, dtype=F32) / HEAD)
    angles = frequency[:, None] * place[None, :]
    cosine, sine = jnp.cos(angles).T, jnp.sin(angles).T
    copies = LANES // HEAD
    return (
        jnp.concatenate([cosine, cosine] * copies, axis=1),
        jnp.concatenate([-sine, sine] * copies, axis=1),
    )


def merge(flows):
    turns = jnp.stack([jnp.int32(0) if bit is None else bit for _, bit in flows]).astype(jnp.int32)
    counts = [len(terms) for terms, _ in flows]
    splits = [bit is not None for _, bit in flows]
    shapes = []
    for (terms, _), split in zip(flows, splits):
        rows = terms[0].shape[0] // (2 if split else 1)
        shapes += [jax.ShapeDtypeStruct((rows, LANES), BF16)] * (2 if split else 1)

    def kernel(turn_ref, *refs):
        ins, outs = refs[:sum(counts)], refs[sum(counts):]
        for n, (count, split) in enumerate(zip(counts, splits)):
            mine, ins = ins[:count], ins[count:]
            for side in range(2 if split else 1):
                out, outs = outs[0], outs[1:]
                rows = out.shape[0]
                if split:
                    part = turn_ref[n] if side == 0 else 1 - turn_ref[n]
                    span = pl.ds(pl.multiple_of(part * rows, 16), rows)
                else:
                    span = pl.ds(0, rows)
                value = mine[0][span, :].astype(F32)
                for ref in mine[1:]:
                    value += ref[span, :].astype(F32)
                out[...] = value.astype(BF16)

    vmem = pl.BlockSpec(memory_space=pltpu.VMEM)
    operands = [term for terms, _ in flows for term in terms]
    size = sum(term.size for term in operands)
    outs = pl.pallas_call(
        kernel,
        in_specs=[pl.BlockSpec(memory_space=pltpu.SMEM)] + [vmem] * len(operands),
        out_specs=[vmem] * len(shapes),
        out_shape=shapes,
        cost_estimate=pl.CostEstimate(flops=size, bytes_accessed=3 * size, transcendentals=0),
    )(turns, *operands)
    result = []
    for split in splits:
        result.append(tuple(outs[:2]) if split else outs[0])
        outs = outs[2 if split else 1:]
    return result


def join(flows):
    turns = jnp.stack([bit for _, _, bit in flows]).astype(jnp.int32)
    shapes = [jax.ShapeDtypeStruct((2 * mine.shape[0], LANES), BF16) for mine, _, _ in flows]

    def kernel(turn_ref, *refs):
        ins, outs = refs[:2 * len(flows)], refs[2 * len(flows):]
        for n, out in enumerate(outs):
            rows = out.shape[0] // 2
            out[pl.ds(pl.multiple_of(turn_ref[n] * rows, 16), rows), :] = ins[2 * n][...]
            out[pl.ds(pl.multiple_of((1 - turn_ref[n]) * rows, 16), rows), :] = ins[2 * n + 1][...]

    vmem = pl.BlockSpec(memory_space=pltpu.VMEM)
    operands = [part for mine, arrived, _ in flows for part in (mine, arrived)]
    size = sum(part.size for part in operands)
    return pl.pallas_call(
        kernel,
        in_specs=[pl.BlockSpec(memory_space=pltpu.SMEM)] + [vmem] * len(operands),
        out_specs=[vmem] * len(shapes),
        out_shape=shapes,
        cost_estimate=pl.CostEstimate(flops=0, bytes_accessed=4 * size, transcendentals=0),
    )(turns, *operands)


def bits(size):
    out, bit = [], 1
    while bit < size:
        out.append(bit)
        bit *= 2
    return out


def swap_with(data, axis, bit):
    size = lax.axis_size(axis)
    return lax.ppermute(data, axis, [(n, n ^ bit) for n in range(size)])


def own_bit(axis, bit):
    return (lax.axis_index(axis) // bit) % 2


def layer(inputs, seq_ids, norm_one, w_qkv, w_out, norm_two, w_gate, w_up, w_down, out_grad):
    dp_bits = [("dp", bit) for bit in bits(lax.axis_size("dp"))]
    stages = len(dp_bits)
    unit = 32 * lax.axis_size("dp")
    width = inputs.shape[1]
    own = jnp.stack([w_gate, w_up, w_down.T])
    side = swap_with(own, "col", 1)
    across = swap_with(own, "row", 1)
    start, place = places(seq_ids)
    start = start[None, :]
    cosine, sine = tables(place)
    gain_one, gain_two = norm_one[None, :], norm_two[None, :]
    q, k, v, lse, attended, middle = front(inputs, start, cosine, sine, gain_one, w_qkv, w_out)
    far = swap_with(side, "row", 1)
    selector = (jnp.arange(16)[:, None] == jnp.arange(width)[None, :] // HEAD).astype(BF16)
    spot = jnp.stack([lax.axis_index("col"), lax.axis_index("row")]).astype(jnp.int32)
    outputs, middle_grad, do, delta, keep_keep, keep_send, send_keep, send_send = mlp(
        unit, spot, middle, out_grad, attended, gain_two, w_out, own, side, across, far, selector
    )
    row_send = swap_with(send_send, "row", 1)
    row_keep = swap_with(send_keep, "row", 1)
    (to_col,) = merge([((keep_send, row_send), None)])
    from_col = swap_with(to_col, "col", 1)
    input_grad, shared_keep, shared_send = back(
        unit, spot, q, k, v, do, lse, delta, start, cosine, sine, inputs, middle_grad, gain_one, w_qkv
    )
    shared_row = swap_with(shared_send, "row", 1)

    half = keep_keep.shape[0] // 2
    order_a = dp_bits
    order_b = dp_bits[1:2] + dp_bits[:1] + dp_bits[2:]
    order_s = [("col", 1)] + dp_bits
    terms = (keep_keep, row_keep, from_col)
    halves = [tuple(term[at:at + half] for term in terms) for at in (0, half)]
    (a, b) = merge([(halves[0], own_bit(*order_a[0])), (halves[1], own_bit(*order_b[0]))])
    (s,) = merge([((shared_keep, shared_row), own_bit(*order_s[0]))])
    for n in range(stages):
        a_in = swap_with(a[1], *order_a[n])
        b_in = swap_with(b[1], *order_b[n])
        s_in = swap_with(s[1], *order_s[n])
        last = n == stages - 1
        a, b, s = merge(
            [
                ((a[0], a_in), None if last else own_bit(*order_a[n + 1])),
                ((b[0], b_in), None if last else own_bit(*order_b[n + 1])),
                ((s[0], s_in), own_bit(*order_s[n + 1])),
            ],
        )
    for n in reversed(range(stages)):
        a_in = swap_with(a, *order_a[n])
        b_in = swap_with(b, *order_b[n])
        pairs = [(a, a_in, own_bit(*order_a[n])), (b, b_in, own_bit(*order_b[n]))]
        if n == stages - 1:
            s_in = swap_with(s[1], *order_s[n + 1])
            (s,) = merge([((s[0], s_in), None)])
        else:
            s_in = swap_with(s, *order_s[n + 2])
            pairs.append((s, s_in, own_bit(*order_s[n + 2])))
        joined = join(pairs)
        a, b = joined[:2]
        if n < stages - 1:
            s = joined[2]
    grads = jnp.concatenate([a, b], axis=0)
    used = 3 * w_gate.size // LANES
    rest = grads[used:]
    for n in (1, 0):
        s_in = swap_with(s, *order_s[n])
        pairs = [(s, s_in, own_bit(*order_s[n]))]
        if n == 0:
            rest_in = swap_with(rest, "col", 1)
            pairs.append((rest, rest_in, own_bit("col", 1)))
        joined = join(pairs)
        s = joined[0]
    rest = joined[1]
    s_in = swap_with(s, "row", 1)
    rest_in = swap_with(rest, "row", 1)
    row_bit = own_bit("row", 1)
    s, rest = join([(s, s_in, row_bit), (rest, rest_in, row_bit)])

    def flat(block, rows):
        return jnp.concatenate([block[at:at + rows] for at in range(0, block.shape[0], rows)], axis=1)

    chunks = padded_width(width) // LANES
    s = s.reshape(2, -1, LANES)
    reach = round_up(w_qkv.shape[1], 2 * LANES) // 2 // LANES * width
    grad_qkv = jnp.concatenate([flat(s[0, :reach], width), flat(s[1, :reach], width)], axis=1)[:, :w_qkv.shape[1]].astype(F32)
    grad_norm_one = jnp.sum(flat(s[0, reach:reach + 16 * chunks], 16)[:8, :width].astype(F32), axis=0)
    rest = rest.reshape(4, -1, LANES)
    quarter = width // 4
    reach = chunks * quarter
    grad_out = jnp.concatenate([flat(rest[n, :reach], quarter)[:, :width] for n in range(4)], axis=0).astype(F32)
    grad_norm_two = jnp.sum(flat(rest[0, reach:reach + 16 * chunks], 16)[:8, :width].astype(F32), axis=0)
    grads = grads[:used].reshape(3, -1, w_gate.shape[0], LANES).astype(F32)
    grad_gate = grads[0].transpose(1, 0, 2).reshape(w_gate.shape)
    grad_up = grads[1].transpose(1, 0, 2).reshape(w_up.shape)
    grad_down = grads[2].transpose(0, 2, 1).reshape(w_down.shape)
    return (outputs, input_grad, grad_norm_one, grad_qkv, grad_out, grad_norm_two, grad_gate, grad_up, grad_down)


def solution(mesh):
    tokens = P(("dp", "row", "col"), None)
    grid, turned = P("col", "row"), P("row", "col")
    return jax.shard_map(
        layer,
        mesh=mesh,
        in_specs=(tokens, P(("dp", "row", "col")), P(), P(), P(), P(), grid, grid, turned, tokens),
        out_specs=(tokens, tokens, P(), P(), P(), P(), grid, grid, turned),
        check_vma=False,
    )
```

```python
import jax
import jax.numpy as jnp
from jax import lax
from jax.experimental import pallas as pl
from jax.experimental.pallas import tpu as pltpu
from jax.sharding import PartitionSpec as P


HEADS = 9
KV_HEADS = 3
GROUP = HEADS // KV_HEADS
HEAD = 64
BLOCK = 256
LANES = 128
LOG2E = 1.4426950408889634
EPS = 1e-05
THETA = 100000.0
NEG = -1e30
F32 = jnp.float32
BF16 = jnp.bfloat16


def dot_nn(a, b):
    return lax.dot_general(a, b, (((1,), (0,)), ((), ())), preferred_element_type=F32)


def dot_nt(a, b):
    return lax.dot_general(a, b, (((1,), (1,)), ((), ())), preferred_element_type=F32)


def dot_tn(a, b):
    return lax.dot_general(a, b, (((0,), (0,)), ((), ())), preferred_element_type=F32)


def partner_lanes(x):
    lane = lax.broadcasted_iota(jnp.int32, x.shape, 1)
    front = lax.rem(lane, HEAD) < HEAD // 2
    return jnp.where(
        front, pltpu.roll(x, LANES - HEAD // 2, 1), pltpu.roll(x, HEAD // 2, 1)
    )


def allowed_tile(start_row, key_start, query_start, diagonal):
    shape = (BLOCK, start_row.shape[1])
    keys = key_start + lax.broadcasted_iota(jnp.int32, shape, 0)
    mask = keys >= start_row
    if diagonal:
        rows = query_start + lax.rem(lax.broadcasted_iota(jnp.int32, shape, 1), BLOCK)
        mask = mask & (keys <= rows)
    return mask


def front_kernel(
    inputs_ref, start_ref, cos_ref, sin_ref, norm_ref, w_qkv_ref, w_out_ref,
    q_ref, k_ref, v_ref, lse_ref, att_ref, mid_ref,
    k_all, vt_all, acc, stat_m, stat_l,
):
    i = pl.program_id(0)
    x = inputs_ref[...].astype(F32)
    scale = lax.rsqrt(jnp.mean(x * x, axis=-1, keepdims=True) + EPS)
    normed = (x * scale * norm_ref[...]).astype(BF16)
    joined = dot_nn(normed, w_qkv_ref[...])
    width = (HEADS + KV_HEADS) * HEAD
    cosine, sine = cos_ref[...], sin_ref[...]
    for c in range(width // LANES):
        part = joined[:, c * LANES:(c + 1) * LANES]
        turned = (part * cosine + partner_lanes(part) * sine).astype(BF16)
        for half in range(2):
            h = 2 * c + half
            piece = turned[:, half * HEAD:(half + 1) * HEAD]
            if h < HEADS:
                q_ref[h] = piece * BF16(HEAD ** -0.5)
            else:
                k_ref[h - HEADS] = piece
                k_all[h - HEADS, pl.ds(pl.multiple_of(i * BLOCK, BLOCK), BLOCK), :] = piece
    values = joined[:, width:]
    values_t = values.T.astype(BF16)
    for g in range(KV_HEADS):
        v_ref[g] = values[:, g * HEAD:(g + 1) * HEAD].astype(BF16)
        vt_all[g, i] = values_t[g * HEAD:(g + 1) * HEAD, :]
    start = start_ref[...]
    start_row = jnp.concatenate([start] * GROUP, axis=1)
    stat_m[...] = jnp.full(stat_m.shape, NEG, F32)
    stat_l[...] = jnp.zeros(stat_l.shape, F32)
    acc[...] = jnp.zeros(acc.shape, F32)

    def tile(j, diagonal):
        mask = allowed_tile(start_row, j * BLOCK, i * BLOCK, diagonal)
        for g in range(KV_HEADS):
            queries = q_ref[g * GROUP:(g + 1) * GROUP].reshape(GROUP * BLOCK, HEAD)
            keys = k_all[g, pl.ds(pl.multiple_of(j * BLOCK, BLOCK), BLOCK), :]
            scores = jnp.where(mask, dot_nt(keys, queries) * LOG2E, NEG)
            peak_old = stat_m[g:g + 1]
            peak = jnp.maximum(peak_old, jnp.max(scores, axis=0, keepdims=True))
            expo = jnp.exp2(scores - peak)
            expo = jnp.where(mask, expo, 0.0)
            fade = jnp.exp2(peak_old - peak)
            stat_m[g:g + 1] = peak
            stat_l[g:g + 1] = stat_l[g:g + 1] * fade + jnp.sum(expo, axis=0, keepdims=True)
            acc[g] = acc[g] * fade + dot_nn(vt_all[g, j], expo.astype(BF16))

    def step(j, carry):
        tile(j, False)
        return carry

    lax.fori_loop(0, i, step, 0)
    tile(i, True)
    pieces = []
    for g in range(KV_HEADS):
        total = stat_l[g:g + 1]
        mixed = acc[g] / total
        logsum = stat_m[g:g + 1] + jnp.log2(total)
        for h in range(GROUP):
            lse_ref[g * GROUP + h:g * GROUP + h + 1, :] = logsum[:, h * BLOCK:(h + 1) * BLOCK]
            pieces.append(mixed[:, h * BLOCK:(h + 1) * BLOCK])
    attended = jnp.concatenate(pieces, axis=0).T.astype(BF16)
    att_ref[...] = attended
    mid_ref[...] = x + dot_nn(attended, w_out_ref[...])


def front(inputs, start, cosine, sine, norm_one, w_qkv, w_out):
    tokens, width = inputs.shape
    blocks = tokens // BLOCK
    whole = lambda i: (0, 0)
    rows = lambda i: (i, 0)
    return pl.pallas_call(
        front_kernel,
        grid=(blocks,),
        in_specs=[
            pl.BlockSpec((BLOCK, width), rows),
            pl.BlockSpec((1, BLOCK), lambda i: (0, i)),
            pl.BlockSpec((BLOCK, LANES), rows),
            pl.BlockSpec((BLOCK, LANES), rows),
            pl.BlockSpec((1, width), whole),
            pl.BlockSpec(w_qkv.shape, whole),
            pl.BlockSpec(w_out.shape, whole),
        ],
        out_specs=[
            pl.BlockSpec((HEADS, BLOCK, HEAD), lambda i: (0, i, 0)),
            pl.BlockSpec((KV_HEADS, BLOCK, HEAD), lambda i: (0, i, 0)),
            pl.BlockSpec((KV_HEADS, BLOCK, HEAD), lambda i: (0, i, 0)),
            pl.BlockSpec((16, BLOCK), lambda i: (0, i)),
            pl.BlockSpec((BLOCK, width), rows),
            pl.BlockSpec((BLOCK, width), rows),
        ],
        out_shape=[
            jax.ShapeDtypeStruct((HEADS, tokens, HEAD), BF16),
            jax.ShapeDtypeStruct((KV_HEADS, tokens, HEAD), BF16),
            jax.ShapeDtypeStruct((KV_HEADS, tokens, HEAD), BF16),
            jax.ShapeDtypeStruct((16, tokens), F32),
            jax.ShapeDtypeStruct((tokens, width), BF16),
            jax.ShapeDtypeStruct((tokens, width), F32),
        ],
        scratch_shapes=[
            pltpu.VMEM((KV_HEADS, tokens, HEAD), BF16),
            pltpu.VMEM((KV_HEADS, blocks, HEAD, BLOCK), BF16),
            pltpu.VMEM((KV_HEADS, HEAD, GROUP * BLOCK), F32),
            pltpu.VMEM((8, GROUP * BLOCK), F32),
            pltpu.VMEM((8, GROUP * BLOCK), F32),
        ],
        cost_estimate=pl.CostEstimate(flops=6 * 10**9, bytes_accessed=12 * 10**6, transcendentals=6 * 10**6),
        name="front",
    )(inputs, start, cosine, sine, norm_one, w_qkv, w_out)


def mlp_kernel(
    place_ref, mid_ref, og_ref, att_ref, norm_ref, w_out_ref, own_ref, side_ref, row_ref, far_ref, sel_ref,
    out_ref, mg_ref, do_ref, delta_ref, g00_ref, g01_ref, g10_ref, g11_ref,
    weights, acc3, acc_out, acc_gain,
):
    i = pl.program_id(0)
    rows_half, cols_half = own_ref.shape[1], own_ref.shape[2]
    col, row = place_ref[0], place_ref[1]

    @pl.when(i == 0)
    def _():
        for ref, c, r in ((own_ref, col, row), (side_ref, 1 - col, row), (row_ref, col, 1 - row), (far_ref, 1 - col, 1 - row)):
            at_row = pl.multiple_of(c * rows_half, 32)
            at_col = pl.multiple_of(r * cols_half, LANES)
            for t in range(3):
                weights[t, pl.ds(at_row, rows_half), pl.ds(at_col, cols_half)] = ref[t]
        acc3[...] = jnp.zeros(acc3.shape, F32)
        acc_out[...] = jnp.zeros(acc_out.shape, F32)
        acc_gain[...] = jnp.zeros(acc_gain.shape, F32)

    middle = mid_ref[...]
    og = og_ref[...]
    gain = norm_ref[...]
    scale = lax.rsqrt(jnp.mean(middle * middle, axis=-1, keepdims=True) + EPS)
    normed = (middle * scale * gain).astype(BF16)
    og_t = og.astype(F32).T.astype(BF16)
    normed_t = normed.astype(F32).T.astype(BF16)
    chunk = cols_half // 2
    mlp_out = jnp.zeros(middle.shape, F32)
    normed_grad = jnp.zeros(middle.shape, F32)
    for c in range(2 * cols_half // chunk):
        at = slice(c * chunk, (c + 1) * chunk)
        gate_pre = dot_nn(normed, weights[0, :, at])
        up_pre = dot_nn(normed, weights[1, :, at])
        hidden_low = dot_nn(og, weights[2, :, at]).astype(BF16).astype(F32)
        squashed = 1.0 / (1.0 + jnp.exp(-gate_pre))
        active = gate_pre * squashed
        hidden = (active * up_pre).astype(BF16)
        gate_low = (hidden_low * up_pre * squashed * (1.0 + gate_pre * (1.0 - squashed))).astype(BF16)
        up_low = (hidden_low * active).astype(BF16)
        mlp_out += dot_nt(hidden, weights[2, :, at])
        normed_grad += dot_nt(gate_low, weights[0, :, at]) + dot_nt(up_low, weights[1, :, at])
        acc3[0, :, at] += dot_nn(normed_t, gate_low)
        acc3[1, :, at] += dot_nn(normed_t, up_low)
        acc3[2, :, at] += dot_nn(og_t, hidden)
    out_ref[...] = (middle + mlp_out).astype(BF16)
    width = middle.shape[1]
    acc_gain[:, :width] += jnp.sum((normed_grad * middle * scale).reshape(BLOCK // 8, 8, width), axis=0)
    weighted = normed_grad * gain
    inner = jnp.sum(weighted * middle, axis=-1, keepdims=True)
    middle_grad = (
        og.astype(F32) + scale * weighted
        - middle * (scale * scale * scale) * inner / middle.shape[1]
    )
    mg_ref[...] = middle_grad
    middle_low = middle_grad.astype(BF16)
    attended = att_ref[...]
    acc_out[:, :width] += dot_tn(attended, middle_low)
    att_low = dot_nt(middle_low, w_out_ref[...]).astype(BF16)
    for h in range(HEADS):
        do_ref[h] = att_low[:, h * HEAD:(h + 1) * HEAD]
    product = att_low.astype(F32) * attended.astype(F32)
    coarse = product.astype(BF16)
    fine = (product - coarse.astype(F32)).astype(BF16)
    delta_ref[...] = dot_nt(sel_ref[...], coarse) + dot_nt(sel_ref[...], fine)

    @pl.when(i == pl.num_programs(0) - 1)
    def _():
        quarter = width // 4
        chunks = acc_out.shape[1] // LANES
        for ref, c, r in ((g00_ref, col, row), (g01_ref, 1 - col, row), (g10_ref, col, 1 - row), (g11_ref, 1 - col, 1 - row)):
            at_row = pl.multiple_of(c * rows_half, 32)
            base = 0
            for t in range(3):
                for part in range(cols_half // LANES):
                    lane = pl.ds(pl.multiple_of(r * cols_half + part * LANES, LANES), LANES)
                    ref[base:base + rows_half, :] = acc3[t, pl.ds(at_row, rows_half), lane].astype(BF16)
                    base += rows_half
            at_row = pl.multiple_of((2 * r + c) * quarter, 16)
            for part in range(chunks):
                at = slice(part * LANES, (part + 1) * LANES)
                ref[base:base + quarter, :] = acc_out[pl.ds(at_row, quarter), at].astype(BF16)
                base += quarter
            share = jnp.where((r == 0) & (c == 0), 1.0, 0.0)
            for part in range(chunks):
                at = slice(part * LANES, (part + 1) * LANES)
                gains = acc_gain[:, at] * share
                ref[base:base + 16, :] = jnp.concatenate([gains, jnp.zeros_like(gains)], axis=0).astype(BF16)
                base += 16
            ref[base:, :] = jnp.zeros((ref.shape[0] - base, LANES), BF16)


def padded_width(width):
    return -(-width // LANES) * LANES


def round_up(count, unit):
    return -(-count // unit) * unit


def mlp(unit, place, middle, out_grad, attended, norm_two, w_out, own, side, across, far, selector):
    tokens, width = middle.shape
    rows_half, cols_half = own.shape[1:]
    blocks = tokens // BLOCK
    chunks = padded_width(width) // LANES
    tall = round_up(3 * cols_half // LANES * rows_half + chunks * (width // 4 + 16), unit)
    block = pl.BlockSpec((tall, LANES), lambda i: (0, 0), pipeline_mode=pl.Buffered(1))
    rows = lambda i: (i, 0)
    whole = lambda i: (0, 0)
    whole3 = lambda i: (0, 0, 0)
    once = pl.Buffered(1)
    return pl.pallas_call(
        mlp_kernel,
        grid=(blocks,),
        in_specs=[
            pl.BlockSpec(memory_space=pltpu.SMEM),
            pl.BlockSpec((BLOCK, width), rows),
            pl.BlockSpec((BLOCK, width), rows),
            pl.BlockSpec((BLOCK, width), rows),
            pl.BlockSpec((1, width), whole),
            pl.BlockSpec(w_out.shape, whole, pipeline_mode=once),
            pl.BlockSpec(own.shape, whole3, pipeline_mode=once),
            pl.BlockSpec(own.shape, whole3, pipeline_mode=once),
            pl.BlockSpec(own.shape, whole3, pipeline_mode=once),
            pl.BlockSpec(own.shape, whole3, pipeline_mode=once),
            pl.BlockSpec(selector.shape, whole),
        ],
        out_specs=[
            pl.BlockSpec((BLOCK, width), rows),
            pl.BlockSpec((BLOCK, width), rows),
            pl.BlockSpec((HEADS, BLOCK, HEAD), lambda i: (0, i, 0)),
            pl.BlockSpec((16, BLOCK), lambda i: (0, i)),
            block, block, block, block,
        ],
        out_shape=[
            jax.ShapeDtypeStruct((tokens, width), BF16),
            jax.ShapeDtypeStruct((tokens, width), F32),
            jax.ShapeDtypeStruct((HEADS, tokens, HEAD), BF16),
            jax.ShapeDtypeStruct((16, tokens), F32),
        ] + [jax.ShapeDtypeStruct((tall, LANES), BF16)] * 4,
        scratch_shapes=[
            pltpu.VMEM((3, 2 * rows_half, 2 * cols_half), BF16),
            pltpu.VMEM((3, 2 * rows_half, 2 * cols_half), F32),
            pltpu.VMEM((width, padded_width(width)), F32),
            pltpu.VMEM((8, padded_width(width)), F32),
        ],
        cost_estimate=pl.CostEstimate(flops=18 * 10**9, bytes_accessed=24 * 10**6, transcendentals=2 * 10**6),
        name="mlp",
    )(place, middle, out_grad, attended, norm_two, w_out, own, side, across, far, selector)


def back_kernel(
    place_ref, q_ref, k_ref, v_ref, do_ref, lse_ref, delta_ref, start_ref, cos_ref, sin_ref,
    inputs_ref, mg_ref, norm_ref, w_qkv_ref,
    ig_ref, keep_ref, send_ref,
    dq_all, dk, dv, acc_qkv, acc_gain,
):
    j = pl.program_id(0)
    blocks = pl.num_programs(0)

    @pl.when(j == 0)
    def _():
        dq_all[...] = jnp.zeros(dq_all.shape, F32)
        acc_qkv[...] = jnp.zeros(acc_qkv.shape, F32)
        acc_gain[...] = jnp.zeros(acc_gain.shape, F32)

    dk[...] = jnp.zeros(dk.shape, F32)
    dv[...] = jnp.zeros(dv.shape, F32)
    keys_t = [k_ref[g].astype(F32).T.astype(BF16) for g in range(KV_HEADS)]

    def tile(i, diagonal):
        at = pl.multiple_of(i * BLOCK, BLOCK)
        span = pl.ds(at, BLOCK)
        start_row = jnp.concatenate([start_ref[:, span]] * GROUP, axis=1)
        mask = allowed_tile(start_row, j * BLOCK, i * BLOCK, diagonal)
        for g in range(KV_HEADS):
            heads = range(g * GROUP, (g + 1) * GROUP)
            queries = q_ref[g * GROUP:(g + 1) * GROUP, span, :].reshape(GROUP * BLOCK, HEAD)
            grads = do_ref[g * GROUP:(g + 1) * GROUP, span, :].reshape(GROUP * BLOCK, HEAD)
            lse_row = jnp.concatenate([lse_ref[h:h + 1, span] for h in heads], axis=1)
            delta_row = jnp.concatenate([delta_ref[h:h + 1, span] for h in heads], axis=1)
            keys, values = k_ref[g], v_ref[g]
            soft = jnp.where(mask, jnp.exp2(dot_nt(keys, queries) * LOG2E - lse_row), 0.0)
            prob_grad = dot_nt(values, grads)
            score_low = (soft * (prob_grad - delta_row)).astype(BF16)
            dv[g] += dot_nn(soft.astype(BF16), grads)
            dk[g] += dot_nn(score_low, queries)
            dq_all[i, g] += dot_nn(keys_t[g], score_low)

    def step(i, carry):
        tile(i, False)
        return carry

    tile(j, True)
    lax.fori_loop(j + 1, blocks, step, 0)

    cosine, sine = cos_ref[...], sin_ref[...]
    pieces = []
    for g in range(KV_HEADS):
        part = dq_all[j, g] * (HEAD ** -0.5)
        pieces += [part[:, h * BLOCK:(h + 1) * BLOCK] for h in range(GROUP)]
    query_grad = jnp.concatenate(pieces, axis=0).T
    turned = jnp.concatenate([query_grad, dk[0], dk[1], dk[2]], axis=1)
    columns = []
    for c in range(turned.shape[1] // LANES):
        part = turned[:, c * LANES:(c + 1) * LANES]
        columns.append((part * cosine - partner_lanes(part) * sine).astype(BF16))
    values_low = jnp.concatenate([dv[0], dv[1], dv[2]], axis=1).astype(BF16)
    joined_low = jnp.concatenate(columns + [values_low], axis=1)

    x = inputs_ref[...].astype(F32)
    gain = norm_ref[...]
    scale = lax.rsqrt(jnp.mean(x * x, axis=-1, keepdims=True) + EPS)
    normed = (x * scale * gain).astype(BF16)
    acc_qkv[:, :joined_low.shape[1]] += dot_tn(normed, joined_low)
    normed_grad = dot_nt(joined_low, w_qkv_ref[...])
    acc_gain[:, :x.shape[1]] += jnp.sum((normed_grad * x * scale).reshape(BLOCK // 8, 8, x.shape[1]), axis=0)
    weighted = normed_grad * gain
    inner = jnp.sum(weighted * x, axis=-1, keepdims=True)
    ig_ref[...] = mg_ref[...] + scale * weighted - x * (scale * scale * scale) * inner / x.shape[1]

    @pl.when(j == blocks - 1)
    def _():
        row = place_ref[1]
        width = x.shape[1]
        half = acc_qkv.shape[1] // 2
        for ref, r in ((keep_ref, row), (send_ref, 1 - row)):
            base = 0
            for part in range(half // LANES):
                lane = pl.ds(pl.multiple_of(r * half + part * LANES, LANES), LANES)
                ref[base:base + width, :] = acc_qkv[:, lane].astype(BF16)
                base += width
            share = jnp.where(r == 0, 1.0, 0.0)
            for part in range(acc_gain.shape[1] // LANES):
                gains = acc_gain[:, part * LANES:(part + 1) * LANES] * share
                ref[base:base + 16, :] = jnp.concatenate([gains, jnp.zeros_like(gains)], axis=0).astype(BF16)
                base += 16
            ref[base:, :] = jnp.zeros((ref.shape[0] - base, LANES), BF16)


def back(unit, place, q, k, v, do, lse, delta, start, cosine, sine, inputs, middle_grad, norm_one, w_qkv):
    tokens, width = inputs.shape
    blocks = tokens // BLOCK
    rows = lambda j: (j, 0)
    whole = lambda j: (0, 0)
    whole3 = lambda j: (0, 0, 0)
    mine3 = lambda j: (0, j, 0)
    wide = round_up(w_qkv.shape[1], 2 * LANES)
    tall = round_up(wide // 2 // LANES * width + 16 * padded_width(width) // LANES, unit)
    block = pl.BlockSpec((tall, LANES), whole)
    return pl.pallas_call(
        back_kernel,
        grid=(blocks,),
        in_specs=[
            pl.BlockSpec(memory_space=pltpu.SMEM),
            pl.BlockSpec(q.shape, whole3),
            pl.BlockSpec((KV_HEADS, BLOCK, HEAD), mine3),
            pl.BlockSpec((KV_HEADS, BLOCK, HEAD), mine3),
            pl.BlockSpec(do.shape, whole3),
            pl.BlockSpec(lse.shape, whole),
            pl.BlockSpec(delta.shape, whole),
            pl.BlockSpec(start.shape, whole),
            pl.BlockSpec((BLOCK, LANES), rows),
            pl.BlockSpec((BLOCK, LANES), rows),
            pl.BlockSpec((BLOCK, width), rows),
            pl.BlockSpec((BLOCK, width), rows),
            pl.BlockSpec((1, width), whole),
            pl.BlockSpec(w_qkv.shape, whole),
        ],
        out_specs=[
            pl.BlockSpec((BLOCK, width), rows),
            block, block,
        ],
        out_shape=[
            jax.ShapeDtypeStruct((tokens, width), F32),
            jax.ShapeDtypeStruct((tall, LANES), BF16),
            jax.ShapeDtypeStruct((tall, LANES), BF16),
        ],
        scratch_shapes=[
            pltpu.VMEM((blocks, KV_HEADS, HEAD, GROUP * BLOCK), F32),
            pltpu.VMEM((KV_HEADS, BLOCK, HEAD), F32),
            pltpu.VMEM((KV_HEADS, BLOCK, HEAD), F32),
            pltpu.VMEM((width, wide), F32),
            pltpu.VMEM((8, padded_width(width)), F32),
        ],
        cost_estimate=pl.CostEstimate(flops=8 * 10**9, bytes_accessed=16 * 10**6, transcendentals=6 * 10**6),
        name="back",
    )(place, q, k, v, do, lse, delta, start, cosine, sine, inputs, middle_grad, norm_one, w_qkv)


def places(seq_ids):
    position = jnp.arange(seq_ids.shape[0], dtype=jnp.int32)
    previous = jnp.concatenate([seq_ids[:1] - 1, seq_ids[:-1]])
    start = lax.cummax(jnp.where(seq_ids != previous, position, 0), axis=0)
    return start, (position - start).astype(F32)


def tables(place):
    half = HEAD // 2
    frequency = THETA ** (-2.0 * jnp.arange(half, dtype=F32) / HEAD)
    angles = frequency[:, None] * place[None, :]
    cosine, sine = jnp.cos(angles).T, jnp.sin(angles).T
    copies = LANES // HEAD
    return (
        jnp.concatenate([cosine, cosine] * copies, axis=1),
        jnp.concatenate([-sine, sine] * copies, axis=1),
    )


VMEM_SPEC = pl.BlockSpec(memory_space=pltpu.VMEM)
SMEM_SPEC = pl.BlockSpec(memory_space=pltpu.SMEM)


def merge(where, flows):
    shapes = []
    for _, _, rows, ways, _ in flows:
        shapes += [jax.ShapeDtypeStruct((rows // ways, LANES), BF16)] * ways
    counts = [len(flow[0]) for flow in flows]

    def kernel(where_ref, *refs):
        ins, outs = refs[:sum(counts)], refs[sum(counts):]
        for terms, first, rows, ways, slot in flows:
            mine, ins = ins[:len(terms)], ins[len(terms):]
            size = rows // ways
            for k in range(ways):
                out, outs = outs[0], outs[1:]
                part = (where_ref[slot] ^ k) if ways > 1 else 0
                span = pl.ds(pl.multiple_of(first + part * size, 16), size)
                value = mine[0][span, :].astype(F32)
                for ref in mine[1:]:
                    value += ref[span, :].astype(F32)
                out[...] = value.astype(BF16)

    operands = [term for flow in flows for term in flow[0]]
    size = sum(flow[2] * LANES * len(flow[0]) for flow in flows)
    outs = pl.pallas_call(
        kernel,
        in_specs=[SMEM_SPEC] + [VMEM_SPEC] * len(operands),
        out_specs=[VMEM_SPEC] * len(shapes),
        out_shape=shapes,
        cost_estimate=pl.CostEstimate(flops=size, bytes_accessed=3 * size, transcendentals=0),
    )(where, *operands)
    result = []
    for flow in flows:
        result.append(list(outs[:flow[3]]))
        outs = outs[flow[3]:]
    return result


def put_parts(where_ref, parts, slot, out, first):
    size = parts[0].shape[0]
    for k, part in enumerate(parts):
        at = first + (where_ref[slot] ^ k) * size
        out[pl.ds(pl.multiple_of(at, 16), size), :] = part[...]


def join(where, flows):
    shapes = [jax.ShapeDtypeStruct((len(parts) * parts[0].shape[0], LANES), BF16) for parts, _ in flows]
    operands = [part for parts, _ in flows for part in parts]

    def kernel(where_ref, *refs):
        ins, outs = refs[:len(operands)], refs[len(operands):]
        for (parts, slot), out in zip(flows, outs):
            put_parts(where_ref, ins[:len(parts)], slot, out, 0)
            ins = ins[len(parts):]

    size = sum(part.size for part in operands)
    return pl.pallas_call(
        kernel,
        in_specs=[SMEM_SPEC] + [VMEM_SPEC] * len(operands),
        out_specs=[VMEM_SPEC] * len(shapes),
        out_shape=shapes,
        cost_estimate=pl.CostEstimate(flops=0, bytes_accessed=4 * size, transcendentals=0),
    )(where, *operands)


def finish_ffn(where, flows, half_shape):
    rows_half, cols_half = half_shape
    operands = [part for parts, _ in flows for part in parts]
    total = sum(part.shape[0] for part in operands)
    used = 3 * rows_half * cols_half // LANES

    def kernel(where_ref, *refs):
        ins = refs[:len(operands)]
        gate_ref, up_ref, down_ref, rest_ref, grads = refs[len(operands):]
        first = 0
        for parts, slot in flows:
            put_parts(where_ref, ins[:len(parts)], slot, grads, first)
            ins = ins[len(parts):]
            first += len(parts) * parts[0].shape[0]
        base = 0
        for t, ref in enumerate((gate_ref, up_ref, down_ref)):
            for part in range(cols_half // LANES):
                tile = grads[base:base + rows_half, :].astype(F32)
                if t < 2:
                    ref[:, part * LANES:(part + 1) * LANES] = tile
                else:
                    ref[part * LANES:(part + 1) * LANES, :] = tile.T
                base += rows_half
        rest_ref[...] = grads[used:, :]

    return pl.pallas_call(
        kernel,
        in_specs=[SMEM_SPEC] + [VMEM_SPEC] * len(operands),
        out_specs=[VMEM_SPEC] * 4,
        out_shape=[
            jax.ShapeDtypeStruct((rows_half, cols_half), F32),
            jax.ShapeDtypeStruct((rows_half, cols_half), F32),
            jax.ShapeDtypeStruct((cols_half, rows_half), F32),
            jax.ShapeDtypeStruct((total - used, LANES), BF16),
        ],
        scratch_shapes=[pltpu.VMEM((total, LANES), BF16)],
        cost_estimate=pl.CostEstimate(flops=0, bytes_accessed=5 * 10**6, transcendentals=0),
    )(where, *operands)


def finish_shared(where, shared, rest, slot, width, columns):
    operands = list(shared) + list(rest)
    chunks = padded_width(width) // LANES
    quarter = width // 4
    per_half = round_up(columns, 2 * LANES) // 2 // LANES

    def kernel(where_ref, s0, s1, r0, r1, qkv_ref, out_ref, one_ref, two_ref, s_all, r_all):
        put_parts(where_ref, (s0, s1), slot, s_all, 0)
        put_parts(where_ref, (r0, r1), slot, r_all, 0)
        half_rows, quarter_rows = s0.shape[0], r0.shape[0] // 2
        for half in range(2):
            for part in range(per_half):
                lane = (half * per_half + part) * LANES
                base = half * half_rows + part * width
                lanes = min(LANES, columns - lane)
                if lanes > 0:
                    qkv_ref[:, lane:lane + lanes] = s_all[base:base + width, :].astype(F32)[:, :lanes]
        for n in range(4):
            for part in range(chunks):
                lanes = min(LANES, width - part * LANES)
                base = n * quarter_rows + part * quarter
                out_ref[n * quarter:(n + 1) * quarter, part * LANES:part * LANES + lanes] = (
                    r_all[base:base + quarter, :].astype(F32)[:, :lanes]
                )
        for ref, source, first in ((one_ref, s_all, per_half * width), (two_ref, r_all, chunks * quarter)):
            for part in range(chunks):
                lanes = min(LANES, width - part * LANES)
                base = first + 16 * part
                total = jnp.sum(source[base:base + 16, :].astype(F32), axis=0, keepdims=True)
                ref[:, part * LANES:part * LANES + lanes] = total[:, :lanes]

    return pl.pallas_call(
        kernel,
        in_specs=[SMEM_SPEC] + [VMEM_SPEC] * 4,
        out_specs=[VMEM_SPEC] * 4,
        out_shape=[
            jax.ShapeDtypeStruct((width, columns), F32),
            jax.ShapeDtypeStruct((width, width), F32),
            jax.ShapeDtypeStruct((1, width), F32),
            jax.ShapeDtypeStruct((1, width), F32),
        ],
        scratch_shapes=[
            pltpu.VMEM((2 * shared[0].shape[0], LANES), BF16),
            pltpu.VMEM((2 * rest[0].shape[0], LANES), BF16),
        ],
        cost_estimate=pl.CostEstimate(flops=0, bytes_accessed=5 * 10**6, transcendentals=0),
    )(where, *operands)


def dp_stages(size):
    masks, bit = [], 1
    while bit < size:
        masks.append(bit)
        bit *= 2
    return [tuple(masks[:1])] + [tuple(masks[n:n + 2]) for n in range(1, len(masks), 2)]


def swap_with(data, axis, mask):
    size = lax.axis_size(axis)
    return lax.ppermute(data, axis, [(n, n ^ mask) for n in range(size)])


def stage_ways(stage):
    return 2 ** len(stage[1])


def stage_mask(stage, k):
    return sum(bit for n, bit in enumerate(stage[1]) if k >> n & 1)


def stage_index(stage):
    index = lax.axis_index(stage[0])
    return sum((index // bit % 2) * 2**n for n, bit in enumerate(stage[1]))


def send_parts(parts, stage):
    return [swap_with(parts[k], stage[0], stage_mask(stage, k)) for k in range(1, stage_ways(stage))]


def spread_part(part, stage):
    return [part] + [swap_with(part, stage[0], stage_mask(stage, k)) for k in range(1, stage_ways(stage))]


def layer(inputs, seq_ids, norm_one, w_qkv, w_out, norm_two, w_gate, w_up, w_down, out_grad):
    unit = 32 * lax.axis_size("dp")
    width = inputs.shape[1]
    col, row = ("col", (1,)), ("row", (1,))
    over_dp = [("dp", masks) for masks in dp_stages(lax.axis_size("dp"))]
    slots = {stage: n for n, stage in enumerate([col, row] + over_dp)}
    own = jnp.stack([w_gate, w_up, w_down.T])
    side = swap_with(own, "col", 1)
    across = swap_with(own, "row", 1)
    start, place = places(seq_ids)
    start = start[None, :]
    cosine, sine = tables(place)
    gain_one, gain_two = norm_one[None, :], norm_two[None, :]
    q, k, v, lse, attended, middle = front(inputs, start, cosine, sine, gain_one, w_qkv, w_out)
    far = swap_with(side, "row", 1)
    selector = (jnp.arange(16)[:, None] == jnp.arange(width)[None, :] // HEAD).astype(BF16)
    where = jnp.stack([stage_index(stage) for stage in slots]).astype(jnp.int32)
    outputs, middle_grad, do, delta, keep_keep, keep_send, send_keep, send_send = mlp(
        unit, where, middle, out_grad, attended, gain_two, w_out, own, side, across, far, selector
    )
    row_send = swap_with(send_send, "row", 1)
    row_keep = swap_with(send_keep, "row", 1)
    tall = keep_keep.shape[0]
    ((to_col,),) = merge(where, [((keep_send, row_send), 0, tall, 1, 0)])
    from_col = swap_with(to_col, "col", 1)
    input_grad, shared_keep, shared_send = back(
        unit, where, q, k, v, do, lse, delta, start, cosine, sine, inputs, middle_grad, gain_one, w_qkv
    )
    shared_row = swap_with(shared_send, "row", 1)

    def flow(terms, first, rows, stage):
        if stage is None:
            return (terms, first, rows, 1, 0)
        return (terms, first, rows, stage_ways(stage), slots[stage])

    order_a = over_dp
    order_b = over_dp[1:2] + over_dp[:1] + over_dp[2:]
    order_s = [col] + over_dp
    count = len(over_dp)
    cut = round_up(2 * tall // 3, unit)
    terms = (keep_keep, row_keep, from_col)
    a, b = merge(where, [flow(terms, 0, cut, order_a[0]), flow(terms, cut, tall - cut, order_b[0])])
    rows_s = shared_keep.shape[0]
    (s,) = merge(where, [flow((shared_keep, shared_row), 0, rows_s, order_s[0])])
    for n in range(count):
        a_in = send_parts(a, order_a[n])
        b_in = send_parts(b, order_b[n])
        s_in = send_parts(s, order_s[n])
        more = n < count - 1
        a, b, s = merge(
            where,
            [
                flow([a[0]] + a_in, 0, a[0].shape[0], order_a[n + 1] if more else None),
                flow([b[0]] + b_in, 0, b[0].shape[0], order_b[n + 1] if more else None),
                flow([s[0]] + s_in, 0, s[0].shape[0], order_s[n + 1]),
            ],
        )
    a, b = a[0], b[0]
    for n in reversed(range(count)):
        a_parts = spread_part(a, order_a[n])
        b_parts = spread_part(b, order_b[n])
        if n == count - 1:
            s_in = send_parts(s, order_s[count])
            ((s,),) = merge(where, [flow([s[0]] + s_in, 0, s[0].shape[0], None)])
        else:
            s_parts = spread_part(s, order_s[n + 2])
        flows = [(a_parts, slots[order_a[n]]), (b_parts, slots[order_b[n]])]
        if n > 0:
            if n < count - 1:
                a, b, s = join(where, flows + [(s_parts, slots[order_s[n + 2]])])
            else:
                a, b = join(where, flows)
        else:
            grad_gate, grad_up, grad_down, rest = finish_ffn(where, flows, w_gate.shape)
            if n < count - 1:
                (s,) = join(where, [(s_parts, slots[order_s[n + 2]])])
    rest_parts = spread_part(rest, col)
    s_parts = spread_part(s, order_s[1])
    (s,) = join(where, [(s_parts, slots[order_s[1]])])
    s_parts = spread_part(s, col)
    s, rest = join(where, [(s_parts, slots[col]), (rest_parts, slots[col])])
    s_parts = spread_part(s, row)
    rest_parts = spread_part(rest, row)
    grad_qkv, grad_out, grad_norm_one, grad_norm_two = finish_shared(
        where, s_parts, rest_parts, slots[row], width, w_qkv.shape[1]
    )
    return (
        outputs, input_grad, grad_norm_one[0], grad_qkv, grad_out, grad_norm_two[0], grad_gate, grad_up, grad_down
    )


def solution(mesh):
    tokens = P(("dp", "row", "col"), None)
    grid, turned = P("col", "row"), P("row", "col")
    return jax.shard_map(
        layer,
        mesh=mesh,
        in_specs=(tokens, P(("dp", "row", "col")), P(), P(), P(), P(), grid, grid, turned, tokens),
        out_specs=(tokens, tokens, P(), P(), P(), P(), grid, grid, turned),
        check_vma=False,
    )
```

```python
import jax
import jax.numpy as jnp
from jax import lax
from jax.experimental import pallas as pl
from jax.experimental.pallas import tpu as pltpu
from jax.sharding import PartitionSpec as P


HEADS = 9
KV_HEADS = 3
GROUP = HEADS // KV_HEADS
HEAD = 64
BLOCK = 256
LANES = 128
LOG2E = 1.4426950408889634
EPS = 1e-05
THETA = 100000.0
NEG = -1e30
F32 = jnp.float32
BF16 = jnp.bfloat16


def dot_nn(a, b):
    return lax.dot_general(a, b, (((1,), (0,)), ((), ())), preferred_element_type=F32)


def dot_nt(a, b):
    return lax.dot_general(a, b, (((1,), (1,)), ((), ())), preferred_element_type=F32)


def dot_tn(a, b):
    return lax.dot_general(a, b, (((0,), (0,)), ((), ())), preferred_element_type=F32)


def partner_lanes(x):
    lane = lax.broadcasted_iota(jnp.int32, x.shape, 1)
    front = lax.rem(lane, HEAD) < HEAD // 2
    return jnp.where(
        front, pltpu.roll(x, LANES - HEAD // 2, 1), pltpu.roll(x, HEAD // 2, 1)
    )


def allowed_tile(start_row, key_start, query_start, diagonal):
    shape = (BLOCK, start_row.shape[1])
    keys = key_start + lax.broadcasted_iota(jnp.int32, shape, 0)
    mask = keys >= start_row
    if diagonal:
        rows = query_start + lax.rem(lax.broadcasted_iota(jnp.int32, shape, 1), BLOCK)
        mask = mask & (keys <= rows)
    return mask


def front_kernel(
    inputs_ref, start_ref, cos_ref, sin_ref, norm_ref, w_qkv_ref, w_out_ref,
    q_ref, k_ref, v_ref, lse_ref, att_ref, mid_ref,
    k_all, vt_all, acc, stat_m, stat_l,
):
    i = pl.program_id(0)
    x = inputs_ref[...].astype(F32)
    scale = lax.rsqrt(jnp.mean(x * x, axis=-1, keepdims=True) + EPS)
    normed = (x * scale * norm_ref[...]).astype(BF16)
    joined = dot_nn(normed, w_qkv_ref[...])
    width = (HEADS + KV_HEADS) * HEAD
    cosine, sine = cos_ref[...], sin_ref[...]
    for c in range(width // LANES):
        part = joined[:, c * LANES:(c + 1) * LANES]
        turned = (part * cosine + partner_lanes(part) * sine).astype(BF16)
        for half in range(2):
            h = 2 * c + half
            piece = turned[:, half * HEAD:(half + 1) * HEAD]
            if h < HEADS:
                q_ref[h] = piece * BF16(HEAD ** -0.5)
            else:
                k_ref[h - HEADS] = piece
                k_all[h - HEADS, pl.ds(pl.multiple_of(i * BLOCK, BLOCK), BLOCK), :] = piece
    values = joined[:, width:]
    values_t = values.T.astype(BF16)
    for g in range(KV_HEADS):
        v_ref[g] = values[:, g * HEAD:(g + 1) * HEAD].astype(BF16)
        vt_all[g, i] = values_t[g * HEAD:(g + 1) * HEAD, :]
    start = start_ref[...]
    start_row = jnp.concatenate([start] * GROUP, axis=1)
    stat_m[...] = jnp.full(stat_m.shape, NEG, F32)
    stat_l[...] = jnp.zeros(stat_l.shape, F32)
    acc[...] = jnp.zeros(acc.shape, F32)

    def tile(j, diagonal):
        mask = allowed_tile(start_row, j * BLOCK, i * BLOCK, diagonal)
        for g in range(KV_HEADS):
            queries = q_ref[g * GROUP:(g + 1) * GROUP].reshape(GROUP * BLOCK, HEAD)
            keys = k_all[g, pl.ds(pl.multiple_of(j * BLOCK, BLOCK), BLOCK), :]
            scores = jnp.where(mask, dot_nt(keys, queries) * LOG2E, NEG)
            peak_old = stat_m[g:g + 1]
            peak = jnp.maximum(peak_old, jnp.max(scores, axis=0, keepdims=True))
            expo = jnp.exp2(scores - peak)
            expo = jnp.where(mask, expo, 0.0)
            fade = jnp.exp2(peak_old - peak)
            stat_m[g:g + 1] = peak
            stat_l[g:g + 1] = stat_l[g:g + 1] * fade + jnp.sum(expo, axis=0, keepdims=True)
            acc[g] = acc[g] * fade + dot_nn(vt_all[g, j], expo.astype(BF16))

    def step(j, carry):
        tile(j, False)
        return carry

    lax.fori_loop(0, i, step, 0)
    tile(i, True)
    pieces = []
    for g in range(KV_HEADS):
        total = stat_l[g:g + 1]
        mixed = acc[g] / total
        logsum = stat_m[g:g + 1] + jnp.log2(total)
        for h in range(GROUP):
            lse_ref[g * GROUP + h:g * GROUP + h + 1, :] = logsum[:, h * BLOCK:(h + 1) * BLOCK]
            pieces.append(mixed[:, h * BLOCK:(h + 1) * BLOCK])
    attended = jnp.concatenate(pieces, axis=0).T.astype(BF16)
    att_ref[...] = attended
    mid_ref[...] = x + dot_nn(attended, w_out_ref[...])


def front(inputs, start, cosine, sine, norm_one, w_qkv, w_out):
    tokens, width = inputs.shape
    blocks = tokens // BLOCK
    whole = lambda i: (0, 0)
    rows = lambda i: (i, 0)
    return pl.pallas_call(
        front_kernel,
        grid=(blocks,),
        in_specs=[
            pl.BlockSpec((BLOCK, width), rows),
            pl.BlockSpec((1, BLOCK), lambda i: (0, i)),
            pl.BlockSpec((BLOCK, LANES), rows),
            pl.BlockSpec((BLOCK, LANES), rows),
            pl.BlockSpec((1, width), whole),
            pl.BlockSpec(w_qkv.shape, whole),
            pl.BlockSpec(w_out.shape, whole),
        ],
        out_specs=[
            pl.BlockSpec((HEADS, BLOCK, HEAD), lambda i: (0, i, 0)),
            pl.BlockSpec((KV_HEADS, BLOCK, HEAD), lambda i: (0, i, 0)),
            pl.BlockSpec((KV_HEADS, BLOCK, HEAD), lambda i: (0, i, 0)),
            pl.BlockSpec((16, BLOCK), lambda i: (0, i)),
            pl.BlockSpec((BLOCK, width), rows),
            pl.BlockSpec((BLOCK, width), rows),
        ],
        out_shape=[
            jax.ShapeDtypeStruct((HEADS, tokens, HEAD), BF16),
            jax.ShapeDtypeStruct((KV_HEADS, tokens, HEAD), BF16),
            jax.ShapeDtypeStruct((KV_HEADS, tokens, HEAD), BF16),
            jax.ShapeDtypeStruct((16, tokens), F32),
            jax.ShapeDtypeStruct((tokens, width), BF16),
            jax.ShapeDtypeStruct((tokens, width), F32),
        ],
        scratch_shapes=[
            pltpu.VMEM((KV_HEADS, tokens, HEAD), BF16),
            pltpu.VMEM((KV_HEADS, blocks, HEAD, BLOCK), BF16),
            pltpu.VMEM((KV_HEADS, HEAD, GROUP * BLOCK), F32),
            pltpu.VMEM((8, GROUP * BLOCK), F32),
            pltpu.VMEM((8, GROUP * BLOCK), F32),
        ],
        cost_estimate=pl.CostEstimate(flops=6 * 10**9, bytes_accessed=12 * 10**6, transcendentals=6 * 10**6),
        name="front",
    )(inputs, start, cosine, sine, norm_one, w_qkv, w_out)


def mlp_kernel(
    place_ref, mid_ref, og_ref, att_ref, norm_ref, w_out_ref, own_ref, side_ref, row_ref, far_ref, sel_ref,
    out_ref, mg_ref, do_ref, delta_ref, g00_ref, g01_ref, g10_ref, g11_ref,
    weights, acc3, acc_out, acc_gain,
):
    i = pl.program_id(0)
    rows_half, cols_half = own_ref.shape[1], own_ref.shape[2]
    col, row = place_ref[0], place_ref[1]

    @pl.when(i == 0)
    def _():
        for ref, c, r in ((own_ref, col, row), (side_ref, 1 - col, row), (row_ref, col, 1 - row), (far_ref, 1 - col, 1 - row)):
            at_row = pl.multiple_of(c * rows_half, 32)
            at_col = pl.multiple_of(r * cols_half, LANES)
            for t in range(3):
                weights[t, pl.ds(at_row, rows_half), pl.ds(at_col, cols_half)] = ref[t]
        acc3[...] = jnp.zeros(acc3.shape, F32)
        acc_out[...] = jnp.zeros(acc_out.shape, F32)
        acc_gain[...] = jnp.zeros(acc_gain.shape, F32)

    middle = mid_ref[...]
    og = og_ref[...]
    gain = norm_ref[...]
    scale = lax.rsqrt(jnp.mean(middle * middle, axis=-1, keepdims=True) + EPS)
    normed = (middle * scale * gain).astype(BF16)
    og_t = og.astype(F32).T.astype(BF16)
    normed_t = normed.astype(F32).T.astype(BF16)
    chunk = cols_half // 2
    mlp_out = jnp.zeros(middle.shape, F32)
    normed_grad = jnp.zeros(middle.shape, F32)
    for c in range(2 * cols_half // chunk):
        at = slice(c * chunk, (c + 1) * chunk)
        gate_pre = dot_nn(normed, weights[0, :, at])
        up_pre = dot_nn(normed, weights[1, :, at])
        hidden_low = dot_nn(og, weights[2, :, at]).astype(BF16).astype(F32)
        squashed = 1.0 / (1.0 + jnp.exp(-gate_pre))
        active = gate_pre * squashed
        hidden = (active * up_pre).astype(BF16)
        gate_low = (hidden_low * up_pre * squashed * (1.0 + gate_pre * (1.0 - squashed))).astype(BF16)
        up_low = (hidden_low * active).astype(BF16)
        mlp_out += dot_nt(hidden, weights[2, :, at])
        normed_grad += dot_nt(gate_low, weights[0, :, at]) + dot_nt(up_low, weights[1, :, at])
        acc3[0, :, at] += dot_nn(normed_t, gate_low)
        acc3[1, :, at] += dot_nn(normed_t, up_low)
        acc3[2, :, at] += dot_nn(og_t, hidden)
    out_ref[...] = (middle + mlp_out).T.astype(BF16)
    width = middle.shape[1]
    acc_gain[:, :width] += jnp.sum((normed_grad * middle * scale).reshape(BLOCK // 8, 8, width), axis=0)
    weighted = normed_grad * gain
    inner = jnp.sum(weighted * middle, axis=-1, keepdims=True)
    middle_grad = (
        og.astype(F32) + scale * weighted
        - middle * (scale * scale * scale) * inner / middle.shape[1]
    )
    mg_ref[...] = middle_grad
    middle_low = middle_grad.astype(BF16)
    attended = att_ref[...]
    acc_out[:, :width] += dot_tn(attended, middle_low)
    att_low = dot_nt(middle_low, w_out_ref[...]).astype(BF16)
    for h in range(HEADS):
        do_ref[h] = att_low[:, h * HEAD:(h + 1) * HEAD]
    product = att_low.astype(F32) * attended.astype(F32)
    coarse = product.astype(BF16)
    fine = (product - coarse.astype(F32)).astype(BF16)
    delta_ref[...] = dot_nt(sel_ref[...], coarse) + dot_nt(sel_ref[...], fine)

    @pl.when(i == pl.num_programs(0) - 1)
    def _():
        quarter = width // 4
        chunks = acc_out.shape[1] // LANES
        for ref, c, r in ((g00_ref, col, row), (g01_ref, 1 - col, row), (g10_ref, col, 1 - row), (g11_ref, 1 - col, 1 - row)):
            at_row = pl.multiple_of(c * rows_half, 32)
            base = 0
            for t in range(3):
                for part in range(cols_half // LANES):
                    lane = pl.ds(pl.multiple_of(r * cols_half + part * LANES, LANES), LANES)
                    ref[base:base + rows_half, :] = acc3[t, pl.ds(at_row, rows_half), lane].astype(BF16)
                    base += rows_half
            at_row = pl.multiple_of((2 * r + c) * quarter, 16)
            for part in range(chunks):
                at = slice(part * LANES, (part + 1) * LANES)
                ref[base:base + quarter, :] = acc_out[pl.ds(at_row, quarter), at].astype(BF16)
                base += quarter
            share = jnp.where((r == 0) & (c == 0), 1.0, 0.0)
            for part in range(chunks):
                at = slice(part * LANES, (part + 1) * LANES)
                gains = acc_gain[:, at] * share
                ref[base:base + 16, :] = jnp.concatenate([gains, jnp.zeros_like(gains)], axis=0).astype(BF16)
                base += 16
            ref[base:, :] = jnp.zeros((ref.shape[0] - base, LANES), BF16)


def padded_width(width):
    return -(-width // LANES) * LANES


def round_up(count, unit):
    return -(-count // unit) * unit


def mlp(unit, place, middle, out_grad, attended, norm_two, w_out, own, side, across, far, selector):
    tokens, width = middle.shape
    rows_half, cols_half = own.shape[1:]
    blocks = tokens // BLOCK
    chunks = padded_width(width) // LANES
    tall = round_up(3 * cols_half // LANES * rows_half + chunks * (width // 4 + 16), unit)
    block = pl.BlockSpec((tall, LANES), lambda i: (0, 0), pipeline_mode=pl.Buffered(1))
    rows = lambda i: (i, 0)
    whole = lambda i: (0, 0)
    whole3 = lambda i: (0, 0, 0)
    once = pl.Buffered(1)
    return pl.pallas_call(
        mlp_kernel,
        grid=(blocks,),
        in_specs=[
            pl.BlockSpec(memory_space=pltpu.SMEM),
            pl.BlockSpec((BLOCK, width), rows),
            pl.BlockSpec((BLOCK, width), rows),
            pl.BlockSpec((BLOCK, width), rows),
            pl.BlockSpec((1, width), whole),
            pl.BlockSpec(w_out.shape, whole, pipeline_mode=once),
            pl.BlockSpec(own.shape, whole3, pipeline_mode=once),
            pl.BlockSpec(own.shape, whole3, pipeline_mode=once),
            pl.BlockSpec(own.shape, whole3, pipeline_mode=once),
            pl.BlockSpec(own.shape, whole3, pipeline_mode=once),
            pl.BlockSpec(selector.shape, whole),
        ],
        out_specs=[
            pl.BlockSpec((width, BLOCK), lambda i: (0, i)),
            pl.BlockSpec((BLOCK, width), rows),
            pl.BlockSpec((HEADS, BLOCK, HEAD), lambda i: (0, i, 0)),
            pl.BlockSpec((16, BLOCK), lambda i: (0, i)),
            block, block, block, block,
        ],
        out_shape=[
            jax.ShapeDtypeStruct((width, tokens), BF16),
            jax.ShapeDtypeStruct((tokens, width), F32),
            jax.ShapeDtypeStruct((HEADS, tokens, HEAD), BF16),
            jax.ShapeDtypeStruct((16, tokens), F32),
        ] + [jax.ShapeDtypeStruct((tall, LANES), BF16)] * 4,
        scratch_shapes=[
            pltpu.VMEM((3, 2 * rows_half, 2 * cols_half), BF16),
            pltpu.VMEM((3, 2 * rows_half, 2 * cols_half), F32),
            pltpu.VMEM((width, padded_width(width)), F32),
            pltpu.VMEM((8, padded_width(width)), F32),
        ],
        cost_estimate=pl.CostEstimate(flops=18 * 10**9, bytes_accessed=24 * 10**6, transcendentals=2 * 10**6),
        name="mlp",
    )(place, middle, out_grad, attended, norm_two, w_out, own, side, across, far, selector)


def back_kernel(
    place_ref, q_ref, k_ref, v_ref, do_ref, lse_ref, delta_ref, start_ref, cos_ref, sin_ref,
    inputs_ref, mg_ref, norm_ref, w_qkv_ref,
    ig_ref, keep_ref, send_ref,
    dq_all, dk, dv, acc_qkv, acc_gain,
):
    j = pl.program_id(0)
    blocks = pl.num_programs(0)

    @pl.when(j == 0)
    def _():
        dq_all[...] = jnp.zeros(dq_all.shape, F32)
        acc_qkv[...] = jnp.zeros(acc_qkv.shape, F32)
        acc_gain[...] = jnp.zeros(acc_gain.shape, F32)

    dk[...] = jnp.zeros(dk.shape, F32)
    dv[...] = jnp.zeros(dv.shape, F32)
    keys_t = [k_ref[g].astype(F32).T.astype(BF16) for g in range(KV_HEADS)]

    def tile(i, diagonal):
        at = pl.multiple_of(i * BLOCK, BLOCK)
        span = pl.ds(at, BLOCK)
        start_row = jnp.concatenate([start_ref[:, span]] * GROUP, axis=1)
        mask = allowed_tile(start_row, j * BLOCK, i * BLOCK, diagonal)
        for g in range(KV_HEADS):
            heads = range(g * GROUP, (g + 1) * GROUP)
            queries = q_ref[g * GROUP:(g + 1) * GROUP, span, :].reshape(GROUP * BLOCK, HEAD)
            grads = do_ref[g * GROUP:(g + 1) * GROUP, span, :].reshape(GROUP * BLOCK, HEAD)
            lse_row = jnp.concatenate([lse_ref[h:h + 1, span] for h in heads], axis=1)
            delta_row = jnp.concatenate([delta_ref[h:h + 1, span] for h in heads], axis=1)
            keys, values = k_ref[g], v_ref[g]
            soft = jnp.where(mask, jnp.exp2(dot_nt(keys, queries) * LOG2E - lse_row), 0.0)
            prob_grad = dot_nt(values, grads)
            score_low = (soft * (prob_grad - delta_row)).astype(BF16)
            dv[g] += dot_nn(soft.astype(BF16), grads)
            dk[g] += dot_nn(score_low, queries)
            dq_all[i, g] += dot_nn(keys_t[g], score_low)

    def step(i, carry):
        tile(i, False)
        return carry

    tile(j, True)
    lax.fori_loop(j + 1, blocks, step, 0)

    cosine, sine = cos_ref[...], sin_ref[...]
    pieces = []
    for g in range(KV_HEADS):
        part = dq_all[j, g] * (HEAD ** -0.5)
        pieces += [part[:, h * BLOCK:(h + 1) * BLOCK] for h in range(GROUP)]
    query_grad = jnp.concatenate(pieces, axis=0).T
    turned = jnp.concatenate([query_grad, dk[0], dk[1], dk[2]], axis=1)
    columns = []
    for c in range(turned.shape[1] // LANES):
        part = turned[:, c * LANES:(c + 1) * LANES]
        columns.append((part * cosine - partner_lanes(part) * sine).astype(BF16))
    values_low = jnp.concatenate([dv[0], dv[1], dv[2]], axis=1).astype(BF16)
    joined_low = jnp.concatenate(columns + [values_low], axis=1)

    x = inputs_ref[...].astype(F32)
    gain = norm_ref[...]
    scale = lax.rsqrt(jnp.mean(x * x, axis=-1, keepdims=True) + EPS)
    normed = (x * scale * gain).astype(BF16)
    acc_qkv[:, :joined_low.shape[1]] += dot_tn(normed, joined_low)
    normed_grad = dot_nt(joined_low, w_qkv_ref[...])
    acc_gain[:, :x.shape[1]] += jnp.sum((normed_grad * x * scale).reshape(BLOCK // 8, 8, x.shape[1]), axis=0)
    weighted = normed_grad * gain
    inner = jnp.sum(weighted * x, axis=-1, keepdims=True)
    input_grad = mg_ref[...] + scale * weighted - x * (scale * scale * scale) * inner / x.shape[1]
    ig_ref[...] = input_grad.T

    @pl.when(j == blocks - 1)
    def _():
        row = place_ref[1]
        width = x.shape[1]
        half = acc_qkv.shape[1] // 2
        for ref, r in ((keep_ref, row), (send_ref, 1 - row)):
            base = 0
            for part in range(half // LANES):
                lane = pl.ds(pl.multiple_of(r * half + part * LANES, LANES), LANES)
                ref[base:base + width, :] = acc_qkv[:, lane].astype(BF16)
                base += width
            share = jnp.where(r == 0, 1.0, 0.0)
            for part in range(acc_gain.shape[1] // LANES):
                gains = acc_gain[:, part * LANES:(part + 1) * LANES] * share
                ref[base:base + 16, :] = jnp.concatenate([gains, jnp.zeros_like(gains)], axis=0).astype(BF16)
                base += 16
            ref[base:, :] = jnp.zeros((ref.shape[0] - base, LANES), BF16)


def back(unit, place, q, k, v, do, lse, delta, start, cosine, sine, inputs, middle_grad, norm_one, w_qkv):
    tokens, width = inputs.shape
    blocks = tokens // BLOCK
    rows = lambda j: (j, 0)
    whole = lambda j: (0, 0)
    whole3 = lambda j: (0, 0, 0)
    mine3 = lambda j: (0, j, 0)
    wide = round_up(w_qkv.shape[1], 2 * LANES)
    tall = round_up(wide // 2 // LANES * width + 16 * padded_width(width) // LANES, unit)
    block = pl.BlockSpec((tall, LANES), whole)
    return pl.pallas_call(
        back_kernel,
        grid=(blocks,),
        in_specs=[
            pl.BlockSpec(memory_space=pltpu.SMEM),
            pl.BlockSpec(q.shape, whole3),
            pl.BlockSpec((KV_HEADS, BLOCK, HEAD), mine3),
            pl.BlockSpec((KV_HEADS, BLOCK, HEAD), mine3),
            pl.BlockSpec(do.shape, whole3),
            pl.BlockSpec(lse.shape, whole),
            pl.BlockSpec(delta.shape, whole),
            pl.BlockSpec(start.shape, whole),
            pl.BlockSpec((BLOCK, LANES), rows),
            pl.BlockSpec((BLOCK, LANES), rows),
            pl.BlockSpec((BLOCK, width), rows),
            pl.BlockSpec((BLOCK, width), rows),
            pl.BlockSpec((1, width), whole),
            pl.BlockSpec(w_qkv.shape, whole),
        ],
        out_specs=[
            pl.BlockSpec((width, BLOCK), lambda j: (0, j)),
            block, block,
        ],
        out_shape=[
            jax.ShapeDtypeStruct((width, tokens), F32),
            jax.ShapeDtypeStruct((tall, LANES), BF16),
            jax.ShapeDtypeStruct((tall, LANES), BF16),
        ],
        scratch_shapes=[
            pltpu.VMEM((blocks, KV_HEADS, HEAD, GROUP * BLOCK), F32),
            pltpu.VMEM((KV_HEADS, BLOCK, HEAD), F32),
            pltpu.VMEM((KV_HEADS, BLOCK, HEAD), F32),
            pltpu.VMEM((width, wide), F32),
            pltpu.VMEM((8, padded_width(width)), F32),
        ],
        cost_estimate=pl.CostEstimate(flops=8 * 10**9, bytes_accessed=16 * 10**6, transcendentals=6 * 10**6),
        name="back",
    )(place, q, k, v, do, lse, delta, start, cosine, sine, inputs, middle_grad, norm_one, w_qkv)


def places(seq_ids):
    position = jnp.arange(seq_ids.shape[0], dtype=jnp.int32)
    previous = jnp.concatenate([seq_ids[:1] - 1, seq_ids[:-1]])
    start = lax.cummax(jnp.where(seq_ids != previous, position, 0), axis=0)
    return start, (position - start).astype(F32)


def tables(place):
    half = HEAD // 2
    frequency = THETA ** (-2.0 * jnp.arange(half, dtype=F32) / HEAD)
    angles = frequency[:, None] * place[None, :]
    cosine, sine = jnp.cos(angles).T, jnp.sin(angles).T
    copies = LANES // HEAD
    return (
        jnp.concatenate([cosine, cosine] * copies, axis=1),
        jnp.concatenate([-sine, sine] * copies, axis=1),
    )


VMEM_SPEC = pl.BlockSpec(memory_space=pltpu.VMEM)
SMEM_SPEC = pl.BlockSpec(memory_space=pltpu.SMEM)


def merge(where, flows):
    shapes = []
    for _, _, rows, ways, _ in flows:
        shapes += [jax.ShapeDtypeStruct((rows // ways, LANES), BF16)] * ways
    counts = [len(flow[0]) for flow in flows]

    def kernel(where_ref, *refs):
        ins, outs = refs[:sum(counts)], refs[sum(counts):]
        for terms, first, rows, ways, slot in flows:
            mine, ins = ins[:len(terms)], ins[len(terms):]
            size = rows // ways
            for k in range(ways):
                out, outs = outs[0], outs[1:]
                part = (where_ref[slot] ^ k) if ways > 1 else 0
                span = pl.ds(pl.multiple_of(first + part * size, 16), size)
                value = mine[0][span, :].astype(F32)
                for ref in mine[1:]:
                    value += ref[span, :].astype(F32)
                out[...] = value.astype(BF16)

    operands = [term for flow in flows for term in flow[0]]
    size = sum(flow[2] * LANES * len(flow[0]) for flow in flows)
    outs = pl.pallas_call(
        kernel,
        in_specs=[SMEM_SPEC] + [VMEM_SPEC] * len(operands),
        out_specs=[VMEM_SPEC] * len(shapes),
        out_shape=shapes,
        cost_estimate=pl.CostEstimate(flops=size, bytes_accessed=3 * size, transcendentals=0),
    )(where, *operands)
    result = []
    for flow in flows:
        result.append(list(outs[:flow[3]]))
        outs = outs[flow[3]:]
    return result


def put_parts(where_ref, parts, slot, out, first):
    size = parts[0].shape[0]
    for k, part in enumerate(parts):
        at = first + (where_ref[slot] ^ k) * size
        out[pl.ds(pl.multiple_of(at, 16), size), :] = part[...]


def join(where, flows):
    shapes = [jax.ShapeDtypeStruct((len(parts) * parts[0].shape[0], LANES), BF16) for parts, _ in flows]
    operands = [part for parts, _ in flows for part in parts]

    def kernel(where_ref, *refs):
        ins, outs = refs[:len(operands)], refs[len(operands):]
        for (parts, slot), out in zip(flows, outs):
            put_parts(where_ref, ins[:len(parts)], slot, out, 0)
            ins = ins[len(parts):]

    size = sum(part.size for part in operands)
    return pl.pallas_call(
        kernel,
        in_specs=[SMEM_SPEC] + [VMEM_SPEC] * len(operands),
        out_specs=[VMEM_SPEC] * len(shapes),
        out_shape=shapes,
        cost_estimate=pl.CostEstimate(flops=0, bytes_accessed=4 * size, transcendentals=0),
    )(where, *operands)


def finish_ffn(where, flows, half_shape):
    rows_half, cols_half = half_shape
    operands = [part for parts, _ in flows for part in parts]
    total = sum(part.shape[0] for part in operands)
    used = 3 * rows_half * cols_half // LANES

    def kernel(where_ref, *refs):
        ins = refs[:len(operands)]
        gate_ref, up_ref, down_ref, rest_ref, grads = refs[len(operands):]
        first = 0
        for parts, slot in flows:
            put_parts(where_ref, ins[:len(parts)], slot, grads, first)
            ins = ins[len(parts):]
            first += len(parts) * parts[0].shape[0]
        base = 0
        for ref in (gate_ref, up_ref, down_ref):
            for part in range(cols_half // LANES):
                tile = grads[base:base + rows_half, :].astype(F32)
                ref[:, part * LANES:(part + 1) * LANES] = tile
                base += rows_half
        rest_ref[...] = grads[used:, :]

    return pl.pallas_call(
        kernel,
        in_specs=[SMEM_SPEC] + [VMEM_SPEC] * len(operands),
        out_specs=[VMEM_SPEC] * 4,
        out_shape=[
            jax.ShapeDtypeStruct((rows_half, cols_half), F32),
            jax.ShapeDtypeStruct((rows_half, cols_half), F32),
            jax.ShapeDtypeStruct((rows_half, cols_half), F32),
            jax.ShapeDtypeStruct((total - used, LANES), BF16),
        ],
        scratch_shapes=[pltpu.VMEM((total, LANES), BF16)],
        cost_estimate=pl.CostEstimate(flops=0, bytes_accessed=5 * 10**6, transcendentals=0),
    )(where, *operands)


def finish_shared(where, shared, rest, slot, width, columns):
    operands = list(shared) + list(rest)
    chunks = padded_width(width) // LANES
    quarter = width // 4
    per_half = round_up(columns, 2 * LANES) // 2 // LANES

    def kernel(where_ref, s0, s1, r0, r1, qkv_ref, out_ref, one_ref, two_ref, s_all, r_all):
        put_parts(where_ref, (s0, s1), slot, s_all, 0)
        put_parts(where_ref, (r0, r1), slot, r_all, 0)
        half_rows, quarter_rows = s0.shape[0], r0.shape[0] // 2
        for half in range(2):
            for part in range(per_half):
                lane = (half * per_half + part) * LANES
                base = half * half_rows + part * width
                lanes = min(LANES, columns - lane)
                if lanes > 0:
                    qkv_ref[:, lane:lane + lanes] = s_all[base:base + width, :].astype(F32)[:, :lanes]
        for n in range(4):
            for part in range(chunks):
                lanes = min(LANES, width - part * LANES)
                base = n * quarter_rows + part * quarter
                out_ref[n * quarter:(n + 1) * quarter, part * LANES:part * LANES + lanes] = (
                    r_all[base:base + quarter, :].astype(F32)[:, :lanes]
                )
        for ref, source, first in ((one_ref, s_all, per_half * width), (two_ref, r_all, chunks * quarter)):
            for part in range(chunks):
                lanes = min(LANES, width - part * LANES)
                base = first + 16 * part
                total = jnp.sum(source[base:base + 16, :].astype(F32), axis=0, keepdims=True)
                ref[:, part * LANES:part * LANES + lanes] = total[:, :lanes]

    return pl.pallas_call(
        kernel,
        in_specs=[SMEM_SPEC] + [VMEM_SPEC] * 4,
        out_specs=[VMEM_SPEC] * 4,
        out_shape=[
            jax.ShapeDtypeStruct((width, columns), F32),
            jax.ShapeDtypeStruct((width, width), F32),
            jax.ShapeDtypeStruct((1, width), F32),
            jax.ShapeDtypeStruct((1, width), F32),
        ],
        scratch_shapes=[
            pltpu.VMEM((2 * shared[0].shape[0], LANES), BF16),
            pltpu.VMEM((2 * rest[0].shape[0], LANES), BF16),
        ],
        cost_estimate=pl.CostEstimate(flops=0, bytes_accessed=5 * 10**6, transcendentals=0),
    )(where, *operands)


def dp_stages(size):
    masks, bit = [], 1
    while bit < size:
        masks.append(bit)
        bit *= 2
    return [tuple(masks[:1])] + [tuple(masks[n:n + 2]) for n in range(1, len(masks), 2)]


def swap_with(data, axis, mask):
    size = lax.axis_size(axis)
    return lax.ppermute(data, axis, [(n, n ^ mask) for n in range(size)])


def stage_ways(stage):
    return 2 ** len(stage[1])


def stage_mask(stage, k):
    return sum(bit for n, bit in enumerate(stage[1]) if k >> n & 1)


def stage_index(stage):
    index = lax.axis_index(stage[0])
    return sum((index // bit % 2) * 2**n for n, bit in enumerate(stage[1]))


def send_parts(parts, stage):
    return [swap_with(parts[k], stage[0], stage_mask(stage, k)) for k in range(1, stage_ways(stage))]


def spread_part(part, stage):
    return [part] + [swap_with(part, stage[0], stage_mask(stage, k)) for k in range(1, stage_ways(stage))]


def layer(inputs, seq_ids, norm_one, w_qkv, w_out, norm_two, w_gate, w_up, w_down, out_grad):
    unit = 32 * lax.axis_size("dp")
    width = inputs.shape[1]
    col, row = ("col", (1,)), ("row", (1,))
    over_dp = [("dp", masks) for masks in dp_stages(lax.axis_size("dp"))]
    slots = {stage: n for n, stage in enumerate([col, row] + over_dp)}
    own = jnp.stack([w_gate, w_up, w_down.T])
    side = swap_with(own, "col", 1)
    across = swap_with(own, "row", 1)
    start, place = places(seq_ids)
    start = start[None, :]
    cosine, sine = tables(place)
    gain_one, gain_two = norm_one[None, :], norm_two[None, :]
    q, k, v, lse, attended, middle = front(inputs, start, cosine, sine, gain_one, w_qkv, w_out)
    far = swap_with(side, "row", 1)
    selector = (jnp.arange(16)[:, None] == jnp.arange(width)[None, :] // HEAD).astype(BF16)
    where = jnp.stack([stage_index(stage) for stage in slots]).astype(jnp.int32)
    outputs, middle_grad, do, delta, keep_keep, keep_send, send_keep, send_send = mlp(
        unit, where, middle, out_grad, attended, gain_two, w_out, own, side, across, far, selector
    )
    row_send = swap_with(send_send, "row", 1)
    row_keep = swap_with(send_keep, "row", 1)
    tall = keep_keep.shape[0]
    ((to_col,),) = merge(where, [((keep_send, row_send), 0, tall, 1, 0)])
    from_col = swap_with(to_col, "col", 1)
    input_grad, shared_keep, shared_send = back(
        unit, where, q, k, v, do, lse, delta, start, cosine, sine, inputs, middle_grad, gain_one, w_qkv
    )
    shared_row = swap_with(shared_send, "row", 1)

    def flow(terms, first, rows, stage):
        if stage is None:
            return (terms, first, rows, 1, 0)
        return (terms, first, rows, stage_ways(stage), slots[stage])

    order_a = over_dp
    order_b = over_dp[1:2] + over_dp[:1] + over_dp[2:]
    order_s = [col] + over_dp
    count = len(over_dp)
    cut = round_up(2 * tall // 3, unit)
    terms = (keep_keep, row_keep, from_col)
    a, b = merge(where, [flow(terms, 0, cut, order_a[0]), flow(terms, cut, tall - cut, order_b[0])])
    rows_s = shared_keep.shape[0]
    (s,) = merge(where, [flow((shared_keep, shared_row), 0, rows_s, order_s[0])])
    for n in range(count):
        a_in = send_parts(a, order_a[n])
        b_in = send_parts(b, order_b[n])
        s_in = send_parts(s, order_s[n])
        more = n < count - 1
        a, b, s = merge(
            where,
            [
                flow([a[0]] + a_in, 0, a[0].shape[0], order_a[n + 1] if more else None),
                flow([b[0]] + b_in, 0, b[0].shape[0], order_b[n + 1] if more else None),
                flow([s[0]] + s_in, 0, s[0].shape[0], order_s[n + 1]),
            ],
        )
    a, b = a[0], b[0]
    for n in reversed(range(count)):
        a_parts = spread_part(a, order_a[n])
        b_parts = spread_part(b, order_b[n])
        if n == count - 1:
            s_in = send_parts(s, order_s[count])
            ((s,),) = merge(where, [flow([s[0]] + s_in, 0, s[0].shape[0], None)])
        else:
            s_parts = spread_part(s, order_s[n + 2])
        flows = [(a_parts, slots[order_a[n]]), (b_parts, slots[order_b[n]])]
        if n > 0:
            if n < count - 1:
                a, b, s = join(where, flows + [(s_parts, slots[order_s[n + 2]])])
            else:
                a, b = join(where, flows)
        else:
            grad_gate, grad_up, grad_down, rest = finish_ffn(where, flows, w_gate.shape)
            if n < count - 1:
                (s,) = join(where, [(s_parts, slots[order_s[n + 2]])])
    rest_parts = spread_part(rest, col)
    s_parts = spread_part(s, order_s[1])
    (s,) = join(where, [(s_parts, slots[order_s[1]])])
    s_parts = spread_part(s, col)
    s, rest = join(where, [(s_parts, slots[col]), (rest_parts, slots[col])])
    s_parts = spread_part(s, row)
    rest_parts = spread_part(rest, row)
    grad_qkv, grad_out, grad_norm_one, grad_norm_two = finish_shared(
        where, s_parts, rest_parts, slots[row], width, w_qkv.shape[1]
    )
    return (
        outputs.T, input_grad.T, grad_norm_one.reshape(width), grad_qkv, grad_out, grad_norm_two.reshape(width),
        grad_gate, grad_up, grad_down.T
    )


def solution(mesh):
    tokens = P(("dp", "row", "col"), None)
    grid, turned = P("col", "row"), P("row", "col")
    return jax.shard_map(
        layer,
        mesh=mesh,
        in_specs=(tokens, P(("dp", "row", "col")), P(), P(), P(), P(), grid, grid, turned, tokens),
        out_specs=(tokens, tokens, P(), P(), P(), P(), grid, grid, turned),
        check_vma=False,
    )
```
